32 devices in a mesh: grp: 2 (over y), stn: 4 (over z), chan: 4 (over x, core).
Axes of the slice: x: 2, y: 2, z: 4, core: 2. Of those that a mesh axis runs over, the one named last changes fastest.
Arguments:
- voltages: bfloat16 [256, 31, 8192], P(('grp', 'stn', 'chan')), parts along dimension 0, may hold values from -6 to 6
- taps: float32 [16, 8192], replicated, may hold values from -1.5 to 1.5
Outputs:
- visibilities: bfloat16 [8, 3, 256, 2, 1024], P(('grp', 'stn'), None, 'chan'), parts along dimension 0
The draws below stay inside these ranges and needn't reach their ends.
There are 2 independent parts, one for each index of `grp`. The reference program is written for one: setup_inputs(seed, part) draws one part's arguments, and reference() takes and returns one part's arrays. A program takes and returns all parts, laid end to end along the dimension named above; an argument that names none is the same for every part. Nothing has to cross between parts.
All inputs are finite; a program needn't handle non-finite values.
Results may differ from the reference program's by a relative error of at most 0.0053.
Values may be sent and summed in bfloat16 or wider, within the bound.
No kernel may reach another device: no remote copies, remote signals or barrier semaphores. Data moves between devices by JAX's collectives and lax.ppermute only.
A program may use at most 64 MiB of HBM per device.

```python
import jax
import jax.numpy as jnp
from jax import lax

CHANNELS = 4096
TAPS = 16
AVG = 16
SPECTRA = 16
IN_DEV = 32
BLOCKS = 4
INPUTS = 128
FRAME_LEN = 8192
FRAMES = 31
REACH = 3
CH_OUT = 256
PAIRS = 1024


def block_levels(stream_key, extent, cuts, least, high):
    def one(dim, parts):
        draws = jax.random.uniform(jax.random.fold_in(jax.random.fold_in(stream_key, 6), dim), (parts,), jnp.float32, least / len(cuts), high / len(cuts))
        return jnp.repeat(jnp.exp(draws), extent[dim] // parts).reshape((-1,) + (1,) * (len(extent) - dim - 1))

    factor_of = one(*cuts[0])
    for cut in cuts[1:]:
        factor_of = factor_of * one(*cut)
    return factor_of


def normal_values(key, dims, spread, bound, split=(), held_as=jnp.bfloat16):
    factor_of = block_levels(key, dims, split, -0.22, 0.18) if split else 1.0
    entries = jax.random.normal(key, dims, jnp.float32) * spread * factor_of
    return jnp.minimum(jnp.maximum(entries, -bound), bound).astype(held_as)


def setup_inputs(seed: int = 0, part: int = 0) -> dict:
    seeds = jax.random.split(jax.random.key(seed), 3)
    part_keys = jax.random.split(jax.random.fold_in(seeds[2], part), 3)
    voltages = normal_values(part_keys[0], (INPUTS, FRAMES, FRAME_LEN), 1.0, 6.0, ((0, 16),))
    taps = normal_values(seeds[1], (TAPS, FRAME_LEN), TAPS ** -0.5, 1.5, (), jnp.float32)
    return dict(voltages=voltages, taps=taps)


def reference(voltages, taps):
    weighted = taps[0] * voltages[:, 0:SPECTRA, :].astype(jnp.float32)
    for tap_index in range(1, TAPS):
        weighted = weighted + taps[tap_index] * voltages[:, tap_index:tap_index + SPECTRA, :].astype(jnp.float32)
    spectrum = jnp.fft.rfft(weighted, axis=-1)[..., :CHANNELS] * (FRAME_LEN ** -0.5)
    real_part = lax.optimization_barrier(jnp.real(spectrum).astype(jnp.bfloat16)).astype(jnp.float32)
    imag_part = lax.optimization_barrier(jnp.imag(spectrum).astype(jnp.bfloat16)).astype(jnp.float32)
    stacked = jnp.concatenate([real_part, imag_part], axis=0)
    stacked = stacked.reshape(2, BLOCKS, IN_DEV, SPECTRA, CH_OUT, AVG)
    stacked = stacked.transpose(1, 4, 0, 2, 3, 5).reshape(BLOCKS, CH_OUT, 2 * IN_DEV, SPECTRA * AVG)
    scale = 1.0 / (SPECTRA * AVG)
    tiles = []
    for distance in range(REACH):
        other = jnp.roll(stacked, -distance, axis=0)
        product = jnp.einsum("ngak,ngck->ngac", stacked, other, precision=lax.Precision.HIGHEST)
        real_vis = product[:, :, :IN_DEV, :IN_DEV] + product[:, :, IN_DEV:, IN_DEV:]
        imag_vis = product[:, :, IN_DEV:, :IN_DEV] - product[:, :, :IN_DEV, IN_DEV:]
        both = jnp.stack([real_vis, imag_vis], axis=2).reshape(BLOCKS, CH_OUT, 2, PAIRS)
        tiles.append((both * scale).astype(jnp.bfloat16))
    return jnp.stack(tiles, axis=1)
```

```python
import functools
import math

import jax
import jax.numpy as jnp
import numpy as np
from jax import lax
from jax.experimental import pallas as pl
from jax.experimental.pallas import tpu as pltpu
from jax.sharding import PartitionSpec as P

AVG = 16
LANES = 128
SUB = 8
f32 = jnp.float32
bf16 = jnp.bfloat16


def add(a, b):
    return b if a is None else a if b is None else a + b


def sub(a, b):
    if b is None:
        return a
    return -b if a is None else a - b


def turn(re, im, num, den):
    num %= den
    if num == 0:
        return re, im
    if 4 * num == den:
        return im, None if re is None else -re
    if 2 * num == den:
        return (None if re is None else -re), (None if im is None else -im)
    if 4 * num == 3 * den:
        return (None if im is None else -im), re
    c = math.cos(2 * math.pi * num / den)
    s = math.sin(2 * math.pi * num / den)
    if 8 * num == den or 8 * num == 5 * den:
        if im is None:
            return re * c, re * -s
        if re is None:
            return im * s, im * c
        return (re + im) * c, (im - re) * c
    if im is None:
        return re * c, re * -s
    if re is None:
        return im * s, im * c
    return re * c + im * s, im * c - re * s


def fft(values, needed):
    size = len(values)
    if size == 1:
        return values
    if all(im is None for _, im in values):
        half_need = size // 4 + 1 if size >= 4 else size // 2
        even = fft(values[0::2], min(half_need, size // 2))
        odd = fft(values[1::2], min(half_need, size // 2))

        def mirrored(part, k):
            n = size // 2
            if k < len(part):
                return part[k]
            re, im = part[n - k]
            return re, (None if im is None else -im)

        out = [None] * size
        for k in range(size // 2):
            if k >= needed and k + size // 2 >= needed:
                continue
            er, ei = mirrored(even, k)
            tr, ti = turn(*mirrored(odd, k), k, size)
            out[k] = (add(er, tr), add(ei, ti))
            out[k + size // 2] = (sub(er, tr), sub(ei, ti))
        return out[:needed]
    even = fft(values[0::2], size // 2)
    odd = fft(values[1::2], size // 2)
    out = [None] * size
    for k in range(size // 2):
        er, ei = even[k]
        tr, ti = turn(*odd[k], k, size)
        out[k] = (add(er, tr), add(ei, ti))
        out[k + size // 2] = (sub(er, tr), sub(ei, ti))
    return out[:needed]


def spectra_kernel(tw_ref, t_ref, x_ref, taps_ref, z_ref, xs_ref, w_ref, a_ref, f_ref, xp_ref, s_ref, *, sizes):
    inputs, frames, tiles, per_step, spectra_count, tap_count = sizes
    half = tiles // 2
    kept = LANES // 2
    rows = (half + 1) * spectra_count
    block = AVG * spectra_count
    parts = tiles // AVG
    step = pl.program_id(0)

    def one_tile(here, carry):
        lanes = pl.ds(pl.multiple_of(here * LANES, LANES), LANES)
        for one in range(inputs):
            xs_ref[pl.ds(one, frames, stride=SUB), :] = x_ref[one, :, lanes].astype(f32)
        weights = [jnp.broadcast_to(taps_ref[t : t + 1, lanes], (SUB, LANES)) for t in range(tap_count)]
        at = (step * per_step + here) * SUB
        for s in range(spectra_count):
            total = weights[0] * xs_ref[s * SUB : (s + 1) * SUB, :]
            for t in range(1, tap_count):
                total = total + weights[t] * xs_ref[(s + t) * SUB : (s + t + 1) * SUB, :]
            w_ref[pl.ds(pl.multiple_of(s * tiles * SUB + at, SUB), SUB), :] = total
        return carry

    lax.fori_loop(0, per_step, one_tile, 0)

    @pl.when(step == pl.num_programs(0) - 1)
    def finish():
        radix = 8
        other = tiles // radix
        columns = radix // 2 + 1

        def one_spectrum(s, carry):
            base = s * tiles * SUB
            present = {}
            for b in range(other):
                got = [
                    (w_ref[pl.ds(pl.multiple_of(base + (other * a + b) * SUB, SUB), SUB), :], None)
                    for a in range(radix)
                ]
                for ka, (re, im) in enumerate(fft(got, columns)):
                    if ka:
                        re, im = turn(re, im, ka * b, tiles)
                    for c, value in enumerate((re, im)):
                        present[ka, b, c] = value is not None
                        if value is not None:
                            at = ((ka * other + b) * 2 + c) * SUB
                            a_ref[at : at + SUB, :] = value
            for ka in range(columns):
                got = []
                for b in range(other):
                    at = (ka * other + b) * 2 * SUB
                    got.append(
                        tuple(
                            a_ref[at + c * SUB : at + (c + 1) * SUB, :] if present[ka, b, c] else None
                            for c in range(2)
                        )
                    )
                need = other if 0 < ka else other // 2 + 1
                done = fft(got, need)
                for kb, (re, im) in enumerate(done):
                    direct = ka + radix * kb
                    if direct <= half:
                        k1, conj = direct, False
                    else:
                        k1, conj = tiles - direct, True
                        if k1 % radix == ka:
                            continue
                    if im is None:
                        im = jnp.zeros_like(re)
                    if conj:
                        im = -im
                    cos = tw_ref[k1 * 2 * SUB : (k1 * 2 + 1) * SUB, :]
                    sin = tw_ref[(k1 * 2 + 1) * SUB : (k1 * 2 + 2) * SUB, :]
                    where = k1 * spectra_count + s
                    f_ref[pl.ds(where, SUB, stride=rows), :] = re * cos + im * sin
                    f_ref[pl.ds(SUB * rows + where, SUB, stride=rows), :] = im * cos - re * sin
            return carry

        lax.fori_loop(0, spectra_count, one_spectrum, 0)

        def one_input(one, carry):
            for c in range(2):
                value = f_ref[pl.ds(pl.multiple_of((c * SUB + one) * rows, SUB), rows), :]
                high = value.astype(bf16)
                xp_ref[:, c * LANES : (c + 1) * LANES] = high
                xp_ref[:, (2 + c) * LANES : (3 + c) * LANES] = (value - high.astype(f32)).astype(bf16)
            for j in range(parts):
                if j < parts // 2:
                    first = j * block
                    which = 0
                else:
                    first = ((parts - 1 - j) * AVG + 1) * spectra_count
                    which = 1
                right = xp_ref[first : first + block, :]
                dims = (((1,), (1,)), ((), ()))
                out = lax.dot_general(
                    t_ref[which, :, : 4 * LANES], right, dims, preferred_element_type=f32
                ) + lax.dot_general(
                    t_ref[which, :, 4 * LANES :], right[:, : 2 * LANES], dims, preferred_element_type=f32
                )
                for c in range(2):
                    for h in range(block // LANES):
                        tile = (j * 2 + c) * (block // LANES) + h
                        s_ref[pl.ds(tile * kept * SUB + one, kept, stride=SUB), :] = out[
                            c * kept : (c + 1) * kept, h * LANES : (h + 1) * LANES
                        ]
            return carry

        lax.fori_loop(0, inputs, one_input, 0)

        wide = 2 * block // LANES

        def one_row(m, carry):
            for j in range(parts):
                for tile in range(wide):
                    at = pl.multiple_of(((j * wide + tile) * kept + m) * SUB, SUB)
                    z_ref[m * parts + j, :, tile * LANES : (tile + 1) * LANES] = s_ref[
                        pl.ds(at, SUB), :
                    ][:inputs].astype(bf16)
            return carry

        lax.fori_loop(0, kept, one_row, 0)


def tables(frame_len):
    tiles = frame_len // LANES
    half = tiles // 2
    kept = LANES // 2
    k1 = np.arange(half + 1)[:, None]
    p = np.arange(LANES)[None, :]
    angle = 2 * np.pi * ((k1 * p) % frame_len) / frame_len
    tw = np.stack([np.cos(angle), np.sin(angle)], axis=1)[:, :, None, :]
    tw = np.broadcast_to(tw, (half + 1, 2, SUB, LANES)).reshape(-1, LANES).astype(np.float32)

    def one(m, sign):
        theta = 2 * np.pi * ((m[:, None] * p) % LANES) / LANES
        cos, sin = np.cos(theta), np.sin(theta)
        full = np.concatenate(
            [np.concatenate([cos, sin], axis=1), sign * np.concatenate([-sin, cos], axis=1)], axis=0
        )
        full = (full * frame_len ** (-0.5)).astype(np.float32)
        high = full.astype(jnp.bfloat16)
        low = (full - high.astype(np.float32)).astype(jnp.bfloat16)
        return np.concatenate([high, high, low], axis=1)

    m = np.arange(kept)
    return tw, np.stack([one(m, 1.0), one(LANES - 1 - m, -1.0)])


def make_spectra(voltages, taps):
    inputs, frames, frame_len = voltages.shape
    tap_count = taps.shape[0]
    spectra_count = frames - tap_count + 1
    tiles = frame_len // LANES
    half = tiles // 2
    rows = (half + 1) * spectra_count
    block = AVG * spectra_count
    groups = frame_len // 2 // AVG
    per_step = 8
    tw, t = tables(frame_len)
    sizes = (inputs, frames, tiles, per_step, spectra_count, tap_count)
    return pl.pallas_call(
        functools.partial(spectra_kernel, sizes=sizes),
        name="spectra",
        grid=(tiles // per_step,),
        in_specs=[
            pl.BlockSpec(tw.shape, lambda q: (0, 0)),
            pl.BlockSpec(t.shape, lambda q: (0, 0, 0)),
            pl.BlockSpec((inputs, frames, per_step * LANES), lambda q: (0, 0, q)),
            pl.BlockSpec((tap_count, per_step * LANES), lambda q: (0, q)),
        ],
        out_specs=pl.BlockSpec((groups, inputs, 2 * block), lambda q: (0, 0, 0)),
        out_shape=jax.ShapeDtypeStruct((groups, inputs, 2 * block), bf16),
        scratch_shapes=[
            pltpu.VMEM(((frames + 1) * SUB, LANES), f32),
            pltpu.VMEM((spectra_count * tiles * SUB, LANES), f32),
            pltpu.VMEM((5 * (tiles // 8) * 2 * SUB, LANES), f32),
            pltpu.VMEM((2 * SUB * rows, LANES), f32),
            pltpu.VMEM((rows, 4 * LANES), bf16),
            pltpu.VMEM((groups * (2 * block // LANES) * SUB, LANES), f32),
        ],
    )(jnp.asarray(tw), jnp.asarray(t), voltages, taps)


def correlate_kernel(r_ref, o_ref, left_ref, right_ref, p_ref, q_ref, *, sizes):
    stations, chans, inputs, reach, scale = sizes
    block_inputs = chans * inputs
    wide = r_ref.shape[-1]
    copies = LANES // block_inputs
    out_rows = block_inputs * block_inputs // LANES
    for b in range(stations):
        own = jnp.concatenate([r_ref[c * stations + b, 0] for c in range(chans)], axis=0)
        at = b * 2 * block_inputs
        left_ref[at : at + block_inputs, :] = own
        left_ref[at + block_inputs : at + 2 * block_inputs, : wide // 2] = own[:, wide // 2 :]
        left_ref[at + block_inputs : at + 2 * block_inputs, wide // 2 :] = -own[:, : wide // 2]
        for r in range(copies):
            right_ref[b * LANES + r * block_inputs : b * LANES + (r + 1) * block_inputs, :] = own
    place = lax.broadcasted_iota(jnp.int32, (out_rows, LANES), 1) // block_inputs

    def one_target(target, carry):
        right = right_ref[pl.ds(pl.multiple_of(target * LANES, LANES), LANES), :]
        for d in range(reach):
            b = lax.rem(target - d + stations, stations)
            left = left_ref[pl.ds(pl.multiple_of(b * 2 * block_inputs, 2 * block_inputs), 2 * block_inputs), :]
            out = lax.dot_general(left, right, (((1,), (1,)), ((), ())), preferred_element_type=f32)
            p_ref[d, :, :] = out * scale
            for part in range(2):
                value = p_ref[d, pl.ds(part * block_inputs, out_rows, stride=copies), :]
                for r in range(1, copies):
                    value = jnp.where(
                        place == r, p_ref[d, pl.ds(part * block_inputs + r, out_rows, stride=copies), :], value
                    )
                q_ref[d, pl.ds(part, out_rows, stride=2), :] = value
            o_ref[b, d, 0, :, :] = q_ref[d].astype(bf16)
        return carry

    lax.fori_loop(0, stations, one_target, 0)


def correlate(turned, stations, chans, reach, scale):
    sources, groups, inputs, wide = turned.shape
    block_inputs = chans * inputs
    out_rows = block_inputs * block_inputs // LANES
    sizes = (stations, chans, inputs, reach, scale)
    return pl.pallas_call(
        functools.partial(correlate_kernel, sizes=sizes),
        name="correlate",
        grid=(groups,),
        in_specs=[pl.BlockSpec((sources, 1, inputs, wide), lambda g: (0, g, 0, 0))],
        out_specs=pl.BlockSpec((stations, reach, 1, 2 * out_rows, LANES), lambda g: (0, 0, g, 0, 0)),
        out_shape=jax.ShapeDtypeStruct((stations, reach, groups, 2 * out_rows, LANES), bf16),
        scratch_shapes=[
            pltpu.VMEM((stations * 2 * block_inputs, wide), bf16),
            pltpu.VMEM((stations * LANES, wide), bf16),
            pltpu.VMEM((reach, 2 * block_inputs, LANES), f32),
            pltpu.VMEM((reach, 2 * out_rows, LANES), f32),
        ],
    )(turned)


def local(voltages, taps):
    inputs_here, frames, frame_len = voltages.shape
    spectra_count = frames - taps.shape[0] + 1
    stations = lax.axis_size("stn")
    chans = lax.axis_size("chan")
    reach = stations // 2 + 1
    block_inputs = chans * inputs_here
    pairs = block_inputs * block_inputs
    spectra = make_spectra(voltages, taps)
    groups, _, wide = spectra.shape
    here = groups // (stations * chans)
    send = spectra.reshape(chans * stations, here, inputs_here, wide)
    turned = lax.all_to_all(send, ("chan", "stn"), 0, 0, tiled=True)
    tiles = correlate(turned, stations, chans, reach, 1.0 / (spectra_count * AVG))
    back = lax.all_to_all(tiles, "stn", 0, 0, tiled=True)
    out = back.transpose(1, 0, 2, 3, 4).reshape(reach, stations * here, pairs // LANES, 2, LANES)
    out = out.transpose(0, 1, 3, 2, 4).reshape(1, reach, stations * here, 2, pairs)
    return out


def solution(mesh):
    placed = (P(("grp", "stn", "chan"), None, None), P())
    return jax.shard_map(
        local,
        mesh=mesh,
        in_specs=placed,
        out_specs=P(("grp", "stn"), None, "chan", None, None),
        check_vma=False,
    )
```

```python
import functools
import math

import jax
import jax.numpy as jnp
import numpy as np
from jax import lax
from jax.experimental import pallas as pl
from jax.experimental.pallas import tpu as pltpu
from jax.sharding import PartitionSpec as P

AVG = 16
LANES = 128
SUB = 8
f32 = jnp.float32
bf16 = jnp.bfloat16


def add(a, b):
    return b if a is None else a if b is None else a + b


def sub(a, b):
    if b is None:
        return a
    return -b if a is None else a - b


def turn(re, im, num, den):
    num %= den
    if num == 0:
        return re, im
    if 4 * num == den:
        return im, None if re is None else -re
    if 2 * num == den:
        return (None if re is None else -re), (None if im is None else -im)
    if 4 * num == 3 * den:
        return (None if im is None else -im), re
    c = math.cos(2 * math.pi * num / den)
    s = math.sin(2 * math.pi * num / den)
    if 8 * num == den or 8 * num == 5 * den:
        if im is None:
            return re * c, re * -s
        if re is None:
            return im * s, im * c
        return (re + im) * c, (im - re) * c
    if im is None:
        return re * c, re * -s
    if re is None:
        return im * s, im * c
    return re * c + im * s, im * c - re * s


def fft(values, needed):
    size = len(values)
    if size == 1:
        return values
    if all(im is None for _, im in values):
        half_need = size // 4 + 1 if size >= 4 else size // 2
        even = fft(values[0::2], min(half_need, size // 2))
        odd = fft(values[1::2], min(half_need, size // 2))

        def mirrored(part, k):
            n = size // 2
            if k < len(part):
                return part[k]
            re, im = part[n - k]
            return re, (None if im is None else -im)

        out = [None] * size
        for k in range(size // 2):
            if k >= needed and k + size // 2 >= needed:
                continue
            er, ei = mirrored(even, k)
            tr, ti = turn(*mirrored(odd, k), k, size)
            out[k] = (add(er, tr), add(ei, ti))
            out[k + size // 2] = (sub(er, tr), sub(ei, ti))
        return out[:needed]
    even = fft(values[0::2], size // 2)
    odd = fft(values[1::2], size // 2)
    out = [None] * size
    for k in range(size // 2):
        er, ei = even[k]
        tr, ti = turn(*odd[k], k, size)
        out[k] = (add(er, tr), add(ei, ti))
        out[k + size // 2] = (sub(er, tr), sub(ei, ti))
    return out[:needed]


def spectra_kernel(tw_ref, t_ref, x_ref, taps_ref, z_ref, xs_ref, w_ref, a_ref, f_ref, xp_ref, s_ref, *, sizes):
    inputs, frames, tiles, per_step, spectra_count, tap_count = sizes
    half = tiles // 2
    kept = LANES // 2
    rows = (half + 1) * spectra_count
    block = AVG * spectra_count
    parts = tiles // AVG
    step = pl.program_id(0)

    def one_tile(here, carry):
        lanes = pl.ds(pl.multiple_of(here * LANES, LANES), LANES)
        for frame in range(frames):
            xs_ref[frame * SUB : frame * SUB + inputs, :] = x_ref[frame, :, lanes].astype(f32)
        weights = [jnp.broadcast_to(taps_ref[t : t + 1, lanes], (SUB, LANES)) for t in range(tap_count)]
        at = (step * per_step + here) * SUB
        for s in range(spectra_count):
            total = weights[0] * xs_ref[s * SUB : (s + 1) * SUB, :]
            for t in range(1, tap_count):
                total = total + weights[t] * xs_ref[(s + t) * SUB : (s + t + 1) * SUB, :]
            w_ref[pl.ds(pl.multiple_of(s * tiles * SUB + at, SUB), SUB), :] = total
        return carry

    lax.fori_loop(0, per_step, one_tile, 0)

    @pl.when(step == pl.num_programs(0) - 1)
    def finish():
        radix = 8
        other = tiles // radix
        columns = radix // 2 + 1

        def one_spectrum(s, carry):
            base = s * tiles * SUB
            present = {}
            for b in range(other):
                got = [
                    (w_ref[pl.ds(pl.multiple_of(base + (other * a + b) * SUB, SUB), SUB), :], None)
                    for a in range(radix)
                ]
                for ka, (re, im) in enumerate(fft(got, columns)):
                    if ka:
                        re, im = turn(re, im, ka * b, tiles)
                    for c, value in enumerate((re, im)):
                        present[ka, b, c] = value is not None
                        if value is not None:
                            at = ((ka * other + b) * 2 + c) * SUB
                            a_ref[at : at + SUB, :] = value
            for ka in range(columns):
                got = []
                for b in range(other):
                    at = (ka * other + b) * 2 * SUB
                    got.append(
                        tuple(
                            a_ref[at + c * SUB : at + (c + 1) * SUB, :] if present[ka, b, c] else None
                            for c in range(2)
                        )
                    )
                need = other if 0 < ka else other // 2 + 1
                done = fft(got, need)
                for kb, (re, im) in enumerate(done):
                    direct = ka + radix * kb
                    if direct <= half:
                        k1, conj = direct, False
                    else:
                        k1, conj = tiles - direct, True
                        if k1 % radix == ka:
                            continue
                    if im is None:
                        im = jnp.zeros_like(re)
                    if conj:
                        im = -im
                    cos = tw_ref[k1 * 2 * SUB : (k1 * 2 + 1) * SUB, :]
                    sin = tw_ref[(k1 * 2 + 1) * SUB : (k1 * 2 + 2) * SUB, :]
                    where = k1 * spectra_count + s
                    f_ref[pl.ds(where, SUB, stride=rows), :] = re * cos + im * sin
                    f_ref[pl.ds(SUB * rows + where, SUB, stride=rows), :] = im * cos - re * sin
            return carry

        lax.fori_loop(0, spectra_count, one_spectrum, 0)

        def one_input(one, carry):
            for c in range(2):
                value = f_ref[pl.ds(pl.multiple_of((c * SUB + one) * rows, SUB), rows), :]
                high = value.astype(bf16)
                xp_ref[:, c * LANES : (c + 1) * LANES] = high
                xp_ref[:, (2 + c) * LANES : (3 + c) * LANES] = (value - high.astype(f32)).astype(bf16)
            for j in range(parts):
                if j < parts // 2:
                    first = j * block
                    which = 0
                else:
                    first = ((parts - 1 - j) * AVG + 1) * spectra_count
                    which = 1
                right = xp_ref[first : first + block, :]
                dims = (((1,), (1,)), ((), ()))
                out = lax.dot_general(
                    t_ref[which, :, : 4 * LANES], right, dims, preferred_element_type=f32
                ) + lax.dot_general(
                    t_ref[which, :, 4 * LANES :], right[:, : 2 * LANES], dims, preferred_element_type=f32
                )
                for c in range(2):
                    for h in range(block // LANES):
                        tile = (j * 2 + c) * (block // LANES) + h
                        s_ref[pl.ds(tile * kept * SUB + one, kept, stride=SUB), :] = out[
                            c * kept : (c + 1) * kept, h * LANES : (h + 1) * LANES
                        ]
            return carry

        lax.fori_loop(0, inputs, one_input, 0)

        wide = 2 * block // LANES

        def one_row(m, carry):
            for j in range(parts):
                for tile in range(wide):
                    at = pl.multiple_of(((j * wide + tile) * kept + m) * SUB, SUB)
                    z_ref[m * parts + j, :, tile * LANES : (tile + 1) * LANES] = s_ref[
                        pl.ds(at, SUB), :
                    ][:inputs].astype(bf16)
            return carry

        lax.fori_loop(0, kept, one_row, 0)


def tables(frame_len):
    tiles = frame_len // LANES
    half = tiles // 2
    kept = LANES // 2
    k1 = np.arange(half + 1)[:, None]
    p = np.arange(LANES)[None, :]
    angle = 2 * np.pi * ((k1 * p) % frame_len) / frame_len
    tw = np.stack([np.cos(angle), np.sin(angle)], axis=1)[:, :, None, :]
    tw = np.broadcast_to(tw, (half + 1, 2, SUB, LANES)).reshape(-1, LANES).astype(np.float32)

    def one(m, sign):
        theta = 2 * np.pi * ((m[:, None] * p) % LANES) / LANES
        cos, sin = np.cos(theta), np.sin(theta)
        full = np.concatenate(
            [np.concatenate([cos, sin], axis=1), sign * np.concatenate([-sin, cos], axis=1)], axis=0
        )
        full = (full * frame_len ** (-0.5)).astype(np.float32)
        high = full.astype(jnp.bfloat16)
        low = (full - high.astype(np.float32)).astype(jnp.bfloat16)
        return np.concatenate([high, high, low], axis=1)

    m = np.arange(kept)
    return tw, np.stack([one(m, 1.0), one(LANES - 1 - m, -1.0)])


def make_spectra(voltages, taps):
    frames, inputs, frame_len = voltages.shape
    tap_count = taps.shape[0]
    spectra_count = frames - tap_count + 1
    tiles = frame_len // LANES
    half = tiles // 2
    rows = (half + 1) * spectra_count
    block = AVG * spectra_count
    groups = frame_len // 2 // AVG
    per_step = 8
    tw, t = tables(frame_len)
    sizes = (inputs, frames, tiles, per_step, spectra_count, tap_count)
    return pl.pallas_call(
        functools.partial(spectra_kernel, sizes=sizes),
        name="spectra",
        grid=(tiles // per_step,),
        in_specs=[
            pl.BlockSpec(tw.shape, lambda q: (0, 0)),
            pl.BlockSpec(t.shape, lambda q: (0, 0, 0)),
            pl.BlockSpec((frames, inputs, per_step * LANES), lambda q: (0, 0, q)),
            pl.BlockSpec((tap_count, per_step * LANES), lambda q: (0, q)),
        ],
        out_specs=pl.BlockSpec((groups, inputs, 2 * block), lambda q: (0, 0, 0)),
        out_shape=jax.ShapeDtypeStruct((groups, inputs, 2 * block), bf16),
        scratch_shapes=[
            pltpu.VMEM(((frames + 1) * SUB, LANES), f32),
            pltpu.VMEM((spectra_count * tiles * SUB, LANES), f32),
            pltpu.VMEM((5 * (tiles // 8) * 2 * SUB, LANES), f32),
            pltpu.VMEM((2 * SUB * rows, LANES), f32),
            pltpu.VMEM((rows, 4 * LANES), bf16),
            pltpu.VMEM((groups * (2 * block // LANES) * SUB, LANES), f32),
        ],
    )(jnp.asarray(tw), jnp.asarray(t), voltages, taps)


def correlate_kernel(r_ref, o_ref, p_ref, q_ref, *, sizes):
    stations, chans, inputs, reach, scale, per_step = sizes
    block_inputs = chans * inputs
    wide = r_ref.shape[-1]
    copies = LANES // block_inputs
    out_rows = block_inputs * block_inputs // LANES
    place = lax.broadcasted_iota(jnp.int32, (out_rows, LANES), 1) // block_inputs

    def fetch(b, g):
        return jnp.concatenate([r_ref[c * stations + b, g] for c in range(chans)], axis=0)

    def lefts(own):
        crossed = jnp.concatenate([own[:, wide // 2 :], -own[:, : wide // 2]], axis=1)
        return [own, crossed]

    def one_target(target, g, blocks, slot):
        right = jnp.concatenate([blocks[0][0]] * copies, axis=0)
        left = jnp.concatenate([piece for pair in blocks for piece in pair], axis=0)
        out = lax.dot_general(left, right, (((1,), (1,)), ((), ())), preferred_element_type=f32)
        p_ref[slot, :, :] = out * scale
        for d in range(reach):
            b = target - d
            b = b % stations if isinstance(b, int) else lax.rem(b + stations, stations)
            for part in range(2):
                base = (2 * d + part) * block_inputs
                value = p_ref[slot, pl.ds(base, out_rows, stride=copies), :]
                for r in range(1, copies):
                    value = jnp.where(place == r, p_ref[slot, pl.ds(base + r, out_rows, stride=copies), :], value)
                q_ref[slot, d, pl.ds(part, out_rows, stride=2), :] = value
            o_ref[b, d, g, :, :] = q_ref[slot, d].astype(bf16)

    for g in range(per_step):
        if stations <= 4:
            pairs = [lefts(fetch(b, g)) for b in range(stations)]
            for target in range(stations):
                one_target(target, g, [pairs[target - d] for d in range(reach)], g * stations + target)
        else:

            def body(target, carry, g=g):
                blocks = [lefts(fetch(lax.rem(target - d + stations, stations), g)) for d in range(reach)]
                one_target(target, g, blocks, 0)
                return carry

            lax.fori_loop(0, stations, body, 0)


def correlate(turned, stations, chans, reach, scale):
    sources, groups, inputs, wide = turned.shape
    block_inputs = chans * inputs
    out_rows = block_inputs * block_inputs // LANES
    per_step = math.gcd(groups, 2)
    sizes = (stations, chans, inputs, reach, scale, per_step)
    slots = per_step * stations if stations <= 4 else 1
    return pl.pallas_call(
        functools.partial(correlate_kernel, sizes=sizes),
        name="correlate",
        grid=(groups // per_step,),
        in_specs=[pl.BlockSpec((sources, per_step, inputs, wide), lambda g: (0, g, 0, 0))],
        out_specs=pl.BlockSpec((stations, reach, per_step, 2 * out_rows, LANES), lambda g: (0, 0, g, 0, 0)),
        out_shape=jax.ShapeDtypeStruct((stations, reach, groups, 2 * out_rows, LANES), bf16),
        scratch_shapes=[
            pltpu.VMEM((slots, reach * 2 * block_inputs, LANES), f32),
            pltpu.VMEM((slots, reach, 2 * out_rows, LANES), f32),
        ],
    )(turned)


def local(voltages, taps):
    inputs_here, frames, frame_len = voltages.shape
    spectra_count = frames - taps.shape[0] + 1
    stations = lax.axis_size("stn")
    chans = lax.axis_size("chan")
    reach = stations // 2 + 1
    block_inputs = chans * inputs_here
    pairs = block_inputs * block_inputs
    spectra = make_spectra(voltages.transpose(1, 0, 2), taps)
    groups, _, wide = spectra.shape
    here = groups // (stations * chans)
    send = spectra.reshape(chans * stations, here, inputs_here, wide)
    turned = lax.all_to_all(send, ("chan", "stn"), 0, 0, tiled=True)
    tiles = correlate(turned, stations, chans, reach, 1.0 / (spectra_count * AVG))
    back = lax.all_to_all(tiles, "stn", 0, 0, tiled=True)
    out = back.transpose(1, 0, 2, 3, 4).reshape(reach, stations * here, pairs // LANES, 2, LANES)
    out = out.transpose(0, 1, 3, 2, 4).reshape(1, reach, stations * here, 2, pairs)
    return out


def solution(mesh):
    placed = (P(("grp", "stn", "chan"), None, None), P())
    return jax.shard_map(
        local,
        mesh=mesh,
        in_specs=placed,
        out_specs=P(("grp", "stn"), None, "chan", None, None),
        check_vma=False,
    )
```

```python
import functools
import math

import jax
import jax.numpy as jnp
import numpy as np
from jax import lax
from jax.experimental import pallas as pl
from jax.experimental.pallas import tpu as pltpu
from jax.sharding import PartitionSpec as P

AVG = 16
LANES = 128
SUB = 8
f32 = jnp.float32
bf16 = jnp.bfloat16


def add(a, b):
    return b if a is None else a if b is None else a + b


def sub(a, b):
    if b is None:
        return a
    return -b if a is None else a - b


def turn(re, im, num, den):
    num %= den
    if num == 0:
        return re, im
    if 4 * num == den:
        return im, None if re is None else -re
    if 2 * num == den:
        return (None if re is None else -re), (None if im is None else -im)
    if 4 * num == 3 * den:
        return (None if im is None else -im), re
    c = math.cos(2 * math.pi * num / den)
    s = math.sin(2 * math.pi * num / den)
    if 8 * num == den or 8 * num == 5 * den:
        if im is None:
            return re * c, re * -s
        if re is None:
            return im * s, im * c
        return (re + im) * c, (im - re) * c
    if im is None:
        return re * c, re * -s
    if re is None:
        return im * s, im * c
    return re * c + im * s, im * c - re * s


def fft(values, needed):
    size = len(values)
    if size == 1:
        return values
    if all(im is None for _, im in values):
        half_need = size // 4 + 1 if size >= 4 else size // 2
        even = fft(values[0::2], min(half_need, size // 2))
        odd = fft(values[1::2], min(half_need, size // 2))

        def mirrored(part, k):
            n = size // 2
            if k < len(part):
                return part[k]
            re, im = part[n - k]
            return re, (None if im is None else -im)

        out = [None] * size
        for k in range(size // 2):
            if k >= needed and k + size // 2 >= needed:
                continue
            er, ei = mirrored(even, k)
            tr, ti = turn(*mirrored(odd, k), k, size)
            out[k] = (add(er, tr), add(ei, ti))
            out[k + size // 2] = (sub(er, tr), sub(ei, ti))
        return out[:needed]
    even = fft(values[0::2], size // 2)
    odd = fft(values[1::2], size // 2)
    out = [None] * size
    for k in range(size // 2):
        er, ei = even[k]
        tr, ti = turn(*odd[k], k, size)
        out[k] = (add(er, tr), add(ei, ti))
        out[k + size // 2] = (sub(er, tr), sub(ei, ti))
    return out[:needed]


def filtered(x, weights, spectra_count):
    tap_count = len(weights)

    def correlated(h, v, count):
        out = []
        for n in range(count):
            total = h[0] * v[n]
            for k in range(1, len(h)):
                total = total + h[k] * v[n + k]
            out.append(total)
        return out

    if tap_count % 2 or spectra_count % 2:
        return correlated(weights, x, spectra_count)
    even, odd = weights[0::2], weights[1::2]
    first, second = x[0::2], x[1::2]
    count = spectra_count // 2
    need = count + tap_count // 2 - 1
    shared = correlated([e + o for e, o in zip(even, odd)], second, count)
    left = correlated(even, [first[n] - second[n] for n in range(need)], count)
    right = correlated(odd, [first[n + 1] - second[n] for n in range(need)], count)
    out = []
    for n in range(count):
        out += [shared[n] + left[n], shared[n] + right[n]]
    return out


SKEW = SUB + 1


def spectra_kernel(place_ref, tw_ref, t_ref, x_ref, taps_ref, *refs, sizes, sends):
    inputs, frames, tiles, per_step, spectra_count, tap_count, stations, chans = sizes
    outs = refs[: len(sends)]
    w_ref, a_ref, f_ref, xp_ref, s_ref, z_ref, sems = refs[len(sends) :]
    half = tiles // 2
    kept = LANES // 2
    rows = (half + 1) * spectra_count
    pitch = rows + 4
    block = AVG * spectra_count
    parts = tiles // AVG
    step = pl.program_id(0)

    def one_tile(here, carry):
        lanes = pl.ds(pl.multiple_of(here * LANES, LANES), LANES)
        x = [x_ref[frame, :, lanes].astype(f32) for frame in range(frames)]
        weights = [jnp.broadcast_to(taps_ref[t : t + 1, lanes], (inputs, LANES)) for t in range(tap_count)]
        at = (step * per_step + here) * SUB
        for s, total in enumerate(filtered(x, weights, spectra_count)):
            w_ref[pl.ds(pl.multiple_of(s * tiles * SUB + at, SUB), inputs), :] = total
        return carry

    lax.fori_loop(0, per_step, one_tile, 0)

    @pl.when(step == pl.num_programs(0) - 1)
    def finish():
        radix = 8
        other = tiles // radix
        columns = radix // 2 + 1

        def one_spectrum(s, carry):
            base = s * tiles * SUB
            present = {}
            for b in range(other):
                got = [
                    (w_ref[pl.ds(pl.multiple_of(base + (other * a + b) * SUB, SUB), SUB), :], None)
                    for a in range(radix)
                ]
                for ka, (re, im) in enumerate(fft(got, columns)):
                    if ka:
                        re, im = turn(re, im, ka * b, tiles)
                    for c, value in enumerate((re, im)):
                        present[ka, b, c] = value is not None
                        if value is not None:
                            at = ((ka * other + b) * 2 + c) * SUB
                            a_ref[at : at + SUB, :] = value
            for ka in range(columns):
                got = []
                for b in range(other):
                    at = (ka * other + b) * 2 * SUB
                    got.append(
                        tuple(
                            a_ref[at + c * SUB : at + (c + 1) * SUB, :] if present[ka, b, c] else None
                            for c in range(2)
                        )
                    )
                need = other if 0 < ka else other // 2 + 1
                done = fft(got, need)
                for kb, (re, im) in enumerate(done):
                    direct = ka + radix * kb
                    if direct <= half:
                        k1, conj = direct, False
                    else:
                        k1, conj = tiles - direct, True
                        if k1 % radix == ka:
                            continue
                    if im is None:
                        im = jnp.zeros_like(re)
                    if conj:
                        im = -im
                    cos = tw_ref[k1 * 2 * SUB : (k1 * 2 + 1) * SUB, :]
                    sin = tw_ref[(k1 * 2 + 1) * SUB : (k1 * 2 + 2) * SUB, :]
                    where = k1 * spectra_count + s
                    f_ref[pl.ds(where, SUB, stride=pitch), :] = re * cos + im * sin
                    f_ref[pl.ds(SUB * pitch + where, SUB, stride=pitch), :] = im * cos - re * sin
            return carry

        lax.fori_loop(0, spectra_count, one_spectrum, 0)

        def one_input(one, carry):
            for c in range(2):
                value = f_ref[pl.ds((c * SUB + one) * pitch, rows), :]
                high = value.astype(bf16)
                xp_ref[:, c * LANES : (c + 1) * LANES] = high
                xp_ref[:, (2 + c) * LANES : (3 + c) * LANES] = (value - high.astype(f32)).astype(bf16)
            for j in range(parts):
                if j < parts // 2:
                    first = j * block
                    which = 0
                else:
                    first = ((parts - 1 - j) * AVG + 1) * spectra_count
                    which = 1
                high = xp_ref[first : first + block, : 2 * LANES]
                low = xp_ref[first : first + block, 2 * LANES :]
                dims = (((1,), (1,)), ((), ()))
                both = lax.dot_general(t_ref[which], high, dims, preferred_element_type=f32)
                more = lax.dot_general(t_ref[which, : 2 * kept], low, dims, preferred_element_type=f32)
                out = both[: 2 * kept] + (both[2 * kept :] + more)
                for c in range(2):
                    for h in range(block // LANES):
                        tile = (j * 2 + c) * (block // LANES) + h
                        s_ref[pl.ds(tile * kept * SKEW + one, kept, stride=SKEW), :] = out[
                            c * kept : (c + 1) * kept, h * LANES : (h + 1) * LANES
                        ]
            return carry

        lax.fori_loop(0, inputs, one_input, 0)

        wide = 2 * block // LANES
        near = math.gcd(kept // chans, 2)

        def staged(m):
            for j in range(parts):
                for tile in range(wide):
                    z_ref[m * parts + j, :, tile * LANES : (tile + 1) * LANES] = s_ref[
                        pl.ds(((j * wide + tile) * kept + m) * SKEW, inputs), :
                    ].astype(bf16)

        copies = []
        for dc in range(chans):
            chan = lax.rem(place_ref[1] + dc, chans)

            def some_rows(at, carry, chan=chan):
                for one in range(near):
                    staged(chan * (kept // chans) + at * near + one)
                return carry

            lax.fori_loop(0, kept // chans // near, some_rows, 0)
            for index, (dz, of, count) in enumerate(sends):
                if of != dc:
                    continue
                first = chan * (kept // chans * parts)
                if dz is not None:
                    first = first + lax.rem(place_ref[0] + dz, stations) * count
                copies.append(
                    pltpu.make_async_copy(z_ref.at[pl.ds(first, count)], outs[index], sems.at[index])
                )
                copies[-1].start()
        for copy in copies:
            copy.wait()


def tables(frame_len):
    tiles = frame_len // LANES
    half = tiles // 2
    kept = LANES // 2
    k1 = np.arange(half + 1)[:, None]
    p = np.arange(LANES)[None, :]
    angle = 2 * np.pi * ((k1 * p) % frame_len) / frame_len
    tw = np.stack([np.cos(angle), np.sin(angle)], axis=1)[:, :, None, :]
    tw = np.broadcast_to(tw, (half + 1, 2, SUB, LANES)).reshape(-1, LANES).astype(np.float32)

    def one(m, sign):
        theta = 2 * np.pi * ((m[:, None] * p) % LANES) / LANES
        cos, sin = np.cos(theta), np.sin(theta)
        full = np.concatenate(
            [np.concatenate([cos, sin], axis=1), sign * np.concatenate([-sin, cos], axis=1)], axis=0
        )
        full = (full * frame_len ** (-0.5)).astype(np.float32)
        high = full.astype(jnp.bfloat16)
        low = (full - high.astype(np.float32)).astype(jnp.bfloat16)
        return np.concatenate([high, low], axis=0)

    m = np.arange(kept)
    return tw, np.stack([one(m, 1.0), one(LANES - 1 - m, -1.0)])


HBM = pl.BlockSpec(memory_space=pl.ANY)


def make_spectra(place, voltages, taps, sends, stations, chans):
    frames, inputs, frame_len = voltages.shape
    tap_count = taps.shape[0]
    spectra_count = frames - tap_count + 1
    tiles = frame_len // LANES
    half = tiles // 2
    rows = (half + 1) * spectra_count
    block = AVG * spectra_count
    groups = frame_len // 2 // AVG
    per_step = 8
    tw, t = tables(frame_len)
    sizes = (inputs, frames, tiles, per_step, spectra_count, tap_count, stations, chans)
    return pl.pallas_call(
        functools.partial(spectra_kernel, sizes=sizes, sends=sends),
        name="spectra",
        grid=(tiles // per_step,),
        in_specs=[
            pl.BlockSpec(memory_space=pltpu.SMEM),
            pl.BlockSpec(tw.shape, lambda q: (0, 0)),
            pl.BlockSpec(t.shape, lambda q: (0, 0, 0)),
            pl.BlockSpec((frames, inputs, per_step * LANES), lambda q: (0, 0, q)),
            pl.BlockSpec((tap_count, per_step * LANES), lambda q: (0, q)),
        ],
        out_specs=[HBM] * len(sends),
        out_shape=[jax.ShapeDtypeStruct((count, inputs, 2 * block), bf16) for _, _, count in sends],
        scratch_shapes=[
            pltpu.VMEM((spectra_count * tiles * SUB, LANES), f32),
            pltpu.VMEM((5 * (tiles // 8) * 2 * SUB, LANES), f32),
            pltpu.VMEM((2 * SUB * (rows + 4), LANES), f32),
            pltpu.VMEM((rows, 4 * LANES), bf16),
            pltpu.VMEM((groups * (2 * block // LANES) * SKEW, LANES), f32),
            pltpu.VMEM((groups, inputs, 2 * block), bf16),
            pltpu.SemaphoreType.DMA((len(sends),)),
        ],
    )(place, jnp.asarray(tw), jnp.asarray(t), voltages, taps)


def lefts(own):
    wide = own.shape[1]
    return [own, jnp.concatenate([own[:, wide // 2 :], -own[:, : wide // 2]], axis=1)]


def tiles_of(blocks, slot, p_ref, q_ref, scale):
    target, rest = blocks
    block_inputs = target.shape[0]
    copies = LANES // block_inputs
    out_rows = block_inputs * block_inputs // LANES
    place = lax.broadcasted_iota(jnp.int32, (out_rows, LANES), 1) // block_inputs
    right = jnp.concatenate([target] * copies, axis=0)
    left = jnp.concatenate([piece for pair in rest for piece in pair], axis=0)
    out = lax.dot_general(left, right, (((1,), (1,)), ((), ())), preferred_element_type=f32)
    p_ref[slot, :, :] = out * scale
    tiles = []
    for d in range(len(rest)):
        for part in range(2):
            base = (2 * d + part) * block_inputs
            value = p_ref[slot, pl.ds(base, out_rows, stride=copies), :]
            for r in range(1, copies):
                value = jnp.where(place == r, p_ref[slot, pl.ds(base + r, out_rows, stride=copies), :], value)
            q_ref[slot, d, pl.ds(part, out_rows, stride=2), :] = value
        tiles.append(q_ref[slot, d].astype(bf16))
    return tiles


def correlate_kernel(r_ref, o_ref, p_ref, q_ref, *, sizes):
    stations, chans, reach, scale = sizes

    def one_target(target, carry):
        owns = []
        for d in range(reach):
            b = lax.rem(target - d + stations, stations)
            owns.append(jnp.concatenate([r_ref[c * stations + b, 0] for c in range(chans)], axis=0))
        tiles = tiles_of((owns[0], [lefts(own) for own in owns]), 0, p_ref, q_ref, scale)
        for d, tile in enumerate(tiles):
            o_ref[lax.rem(target - d + stations, stations), d, 0, :, :] = tile
        return carry

    lax.fori_loop(0, stations, one_target, 0)


def correlate(turned, stations, chans, reach, scale):
    sources, groups, inputs, wide = turned.shape
    block_inputs = chans * inputs
    out_rows = block_inputs * block_inputs // LANES
    return pl.pallas_call(
        functools.partial(correlate_kernel, sizes=(stations, chans, reach, scale)),
        name="correlate",
        grid=(groups,),
        in_specs=[pl.BlockSpec((sources, 1, inputs, wide), lambda g: (0, g, 0, 0))],
        out_specs=pl.BlockSpec((stations, reach, 1, 2 * out_rows, LANES), lambda g: (0, 0, g, 0, 0)),
        out_shape=jax.ShapeDtypeStruct((stations, reach, groups, 2 * out_rows, LANES), bf16),
        scratch_shapes=[
            pltpu.VMEM((1, reach * 2 * block_inputs, LANES), f32),
            pltpu.VMEM((1, reach, 2 * out_rows, LANES), f32),
        ],
    )(turned)


def pieces_kernel(place_ref, *refs, sizes, pieces):
    blocks, chans, groups, distances, scale, per_step = sizes
    arrived = refs[: len(pieces)]
    outs = refs[len(pieces) : len(pieces) + blocks]
    r_ref, p_ref, q_ref, sems = refs[len(pieces) + blocks :]
    copies = []
    for index, (block, dc, mine, first) in enumerate(pieces):
        chan = lax.rem(place_ref[1] - dc + chans, chans)
        start = first + place_ref[0] * mine if mine else first
        copies.append(
            pltpu.make_async_copy(
                arrived[index].at[pl.ds(start, groups)], r_ref.at[block * chans + chan], sems.at[index]
            )
        )
        copies[-1].start()
    for copy in copies:
        copy.wait()

    def some_groups(at, carry):
        for one in range(per_step):
            g = at * per_step + one
            owns = [
                jnp.concatenate([r_ref[block * chans + c, g] for c in range(chans)], axis=0)
                for block in range(blocks)
            ]
            pairs = [lefts(own) for own in owns]
            for target in range(blocks):
                who = [(target - d) % blocks for d in distances]
                tiles = tiles_of(
                    (owns[target], [pairs[b] for b in who]), one * blocks + target, p_ref, q_ref, scale
                )
                for d, (b, tile) in enumerate(zip(who, tiles)):
                    outs[b][d, g, :, :] = tile
        return carry

    lax.fori_loop(0, groups // per_step, some_groups, 0)


def correlate_pieces(place, arrays, pieces, blocks, chans, groups, distances, scale, name):
    inputs, wide = arrays[0].shape[1:]
    block_inputs = chans * inputs
    out_rows = block_inputs * block_inputs // LANES
    per_step = math.gcd(groups, 8 // blocks)
    sizes = (blocks, chans, groups, distances, scale, per_step)
    shape = (len(distances), groups, 2 * out_rows, LANES)
    vmem = pl.BlockSpec(memory_space=pltpu.VMEM)
    return pl.pallas_call(
        functools.partial(pieces_kernel, sizes=sizes, pieces=pieces),
        name=name,
        in_specs=[pl.BlockSpec(memory_space=pltpu.SMEM)] + [HBM] * len(arrays),
        out_specs=[vmem] * blocks,
        out_shape=[jax.ShapeDtypeStruct(shape, bf16)] * blocks,
        scratch_shapes=[
            pltpu.VMEM((blocks * chans, groups, inputs, wide), bf16),
            pltpu.VMEM((per_step * blocks, len(distances) * 2 * block_inputs, LANES), f32),
            pltpu.VMEM((per_step * blocks, len(distances), 2 * out_rows, LANES), f32),
            pltpu.SemaphoreType.DMA((len(pieces),)),
        ],
    )(place, *arrays)


def assemble_kernel(place_ref, own_ref, *refs, stations, chunks):
    parts = refs[: stations * chunks]
    out_ref = refs[stations * chunks]
    sems = refs[stations * chunks + 1]
    copies = []
    for dz in range(stations):
        host = lax.rem(place_ref[0] - dz + stations, stations)
        for chunk in range(chunks):
            part = parts[dz * chunks + chunk]
            for d in range(part.shape[0]):
                count = part.shape[1]
                at = (host * chunks + chunk) * count
                copies.append(
                    pltpu.make_async_copy(part.at[d], out_ref.at[d + 1, pl.ds(at, count)], sems.at[len(copies)])
                )
                copies[-1].start()
    copies.append(pltpu.make_async_copy(own_ref.at[0], out_ref.at[0], sems.at[len(copies)]))
    copies[-1].start()
    for copy in copies:
        copy.wait()


def assemble(place, own, parts, stations, chunks):
    reach = parts[0].shape[0] + 1
    return pl.pallas_call(
        functools.partial(assemble_kernel, stations=stations, chunks=chunks),
        name="assemble",
        in_specs=[pl.BlockSpec(memory_space=pltpu.SMEM)] + [HBM] * (1 + len(parts)),
        out_specs=HBM,
        out_shape=jax.ShapeDtypeStruct((reach,) + own.shape[1:], bf16),
        scratch_shapes=[pltpu.SemaphoreType.DMA((len(parts) * (reach - 1) + 1,))],
    )(place, own, *parts)


def shifted(value, stations, chans, dz, dc):
    pairs = [
        (z * chans + c, (z + dz) % stations * chans + (c + dc) % chans)
        for z in range(stations)
        for c in range(chans)
    ]
    return lax.ppermute(value, ("stn", "chan"), pairs)


def local(voltages, taps):
    inputs_here, frames, frame_len = voltages.shape
    spectra_count = frames - taps.shape[0] + 1
    stations = lax.axis_size("stn")
    chans = lax.axis_size("chan")
    reach = stations // 2 + 1
    block_inputs = chans * inputs_here
    pairs = block_inputs * block_inputs
    groups = frame_len // 2 // AVG
    here = groups // (stations * chans)
    scale = 1.0 / (spectra_count * AVG)
    place = jnp.stack([lax.axis_index("stn"), lax.axis_index("chan")]).astype(jnp.int32)
    frames_first = voltages.transpose(1, 0, 2)
    if stations * chans > 16 or reach > stations:
        sends = tuple((None, dc, groups // chans) for dc in range(chans))
        still = jnp.zeros_like(place)
        slices = make_spectra(still, frames_first, taps, sends, stations, chans)
        send = jnp.concatenate(slices, axis=0).reshape(chans * stations, here, inputs_here, -1)
        turned = lax.all_to_all(send, ("chan", "stn"), 0, 0, tiled=True)
        tiles = correlate(turned, stations, chans, reach, scale)
        back = lax.all_to_all(tiles, "stn", 0, 0, tiled=True)
        out = back.transpose(1, 0, 2, 3, 4)
    else:
        sends = tuple((None, dc, here * stations) for dc in range(chans)) + tuple(
            (dz, dc, here) for dz in range(1, stations) for dc in range(chans)
        )
        sent = make_spectra(place, frames_first, taps, sends, stations, chans)
        got = {}
        for (dz, dc, _), value in zip(sends, sent):
            move = dz or 0
            got[dz, dc] = value if move == 0 and dc == 0 else shifted(value, stations, chans, move, dc)
        whole = [got[None, dc] for dc in range(chans)]
        (own,) = correlate_pieces(
            place, whole, [(0, dc, 0, 0) for dc in range(chans)], 1, chans, here * stations, (0,), scale, "own"
        )
        chunks = 2
        part = here // chunks
        distances = tuple(range(1, reach))
        back = {}
        for chunk in range(chunks):
            pieces = [(0, dc, here, chunk * part) for dc in range(chans)]
            arrays = list(whole)
            for dz in range(1, stations):
                for dc in range(chans):
                    pieces.append((-dz % stations, dc, 0, chunk * part))
                    arrays.append(got[dz, dc])
            outs = correlate_pieces(
                place, arrays, pieces, stations, chans, part, distances, scale, "cross"
            )
            for dz in range(stations):
                back[dz, chunk] = outs[0] if dz == 0 else shifted(outs[dz], stations, chans, dz, 0)
        out = assemble(
            place, own, [back[dz, chunk] for dz in range(stations) for chunk in range(chunks)], stations, chunks
        )
    out = out.reshape(reach, stations * here, pairs // LANES, 2, LANES)
    return out.transpose(0, 1, 3, 2, 4).reshape(1, reach, stations * here, 2, pairs)


def solution(mesh):
    placed = (P(("grp", "stn", "chan"), None, None), P())
    return jax.shard_map(
        local,
        mesh=mesh,
        in_specs=placed,
        out_specs=P(("grp", "stn"), None, "chan", None, None),
        check_vma=False,
    )
```

```python
import functools
import math

import jax
import jax.numpy as jnp
import numpy as np
from jax import lax
from jax.experimental import pallas as pl
from jax.experimental.pallas import tpu as pltpu
from jax.sharding import PartitionSpec as P


AVG = 16
LANES = 128
SUB = 8
f32 = jnp.float32
bf16 = jnp.bfloat16


def add(a, b):
    return b if a is None else a if b is None else a + b


def sub(a, b):
    if b is None:
        return a
    return -b if a is None else a - b


def turn(re, im, num, den):
    num %= den
    if num == 0:
        return re, im
    if 4 * num == den:
        return im, None if re is None else -re
    if 2 * num == den:
        return (None if re is None else -re), (None if im is None else -im)
    if 4 * num == 3 * den:
        return (None if im is None else -im), re
    c = math.cos(2 * math.pi * num / den)
    s = math.sin(2 * math.pi * num / den)
    if 8 * num == den or 8 * num == 5 * den:
        if im is None:
            return re * c, re * -s
        if re is None:
            return im * s, im * c
        return (re + im) * c, (im - re) * c
    if im is None:
        return re * c, re * -s
    if re is None:
        return im * s, im * c
    return re * c + im * s, im * c - re * s


def fft(values, needed):
    size = len(values)
    if size == 1:
        return values
    if all(im is None for _, im in values):
        half_need = size // 4 + 1 if size >= 4 else size // 2
        even = fft(values[0::2], min(half_need, size // 2))
        odd = fft(values[1::2], min(half_need, size // 2))

        def mirrored(part, k):
            n = size // 2
            if k < len(part):
                return part[k]
            re, im = part[n - k]
            return re, (None if im is None else -im)

        out = [None] * size
        for k in range(size // 2):
            if k >= needed and k + size // 2 >= needed:
                continue
            er, ei = mirrored(even, k)
            tr, ti = turn(*mirrored(odd, k), k, size)
            out[k] = (add(er, tr), add(ei, ti))
            out[k + size // 2] = (sub(er, tr), sub(ei, ti))
        return out[:needed]
    even = fft(values[0::2], size // 2)
    odd = fft(values[1::2], size // 2)
    out = [None] * size
    for k in range(size // 2):
        er, ei = even[k]
        tr, ti = turn(*odd[k], k, size)
        out[k] = (add(er, tr), add(ei, ti))
        out[k + size // 2] = (sub(er, tr), sub(ei, ti))
    return out[:needed]


def filtered(x, weights, spectra_count):
    tap_count = len(weights)

    def correlated(h, v, count):
        out = []
        for n in range(count):
            total = h[0] * v[n]
            for k in range(1, len(h)):
                total = total + h[k] * v[n + k]
            out.append(total)
        return out

    if tap_count % 2 or spectra_count % 2:
        return correlated(weights, x, spectra_count)
    even, odd = weights[0::2], weights[1::2]
    first, second = x[0::2], x[1::2]
    count = spectra_count // 2
    need = count + tap_count // 2 - 1
    shared = correlated([e + o for e, o in zip(even, odd)], second, count)
    left = correlated(even, [first[n] - second[n] for n in range(need)], count)
    right = correlated(odd, [first[n + 1] - second[n] for n in range(need)], count)
    out = []
    for n in range(count):
        out += [shared[n] + left[n], shared[n] + right[n]]
    return out


SKEW = SUB + 1


def spectra_kernel(tw_ref, t_ref, x_ref, taps_ref, *refs, sizes, sends, turned):
    inputs, frames, tiles, per_step, spectra_count, tap_count, stations, chans = sizes
    outs = refs[: len(sends)]
    w_ref, a_ref, f_ref, xp_ref, s_ref, z_ref, sems = refs[len(sends) :]
    half = tiles // 2
    kept = LANES // 2
    rows = (half + 1) * spectra_count
    pitch = rows + 4
    block = AVG * spectra_count
    parts = tiles // AVG
    step = pl.program_id(0)

    def one_tile(here, carry):
        lanes = pl.ds(pl.multiple_of(here * LANES, LANES), LANES)
        x = [x_ref[frame, :, lanes].astype(f32) for frame in range(frames)]
        weights = [jnp.broadcast_to(taps_ref[t : t + 1, lanes], (inputs, LANES)) for t in range(tap_count)]
        at = (step * per_step + here) * SUB
        for s, total in enumerate(filtered(x, weights, spectra_count)):
            w_ref[pl.ds(pl.multiple_of(s * tiles * SUB + at, SUB), inputs), :] = total
        return carry

    lax.fori_loop(0, per_step, one_tile, 0)

    @pl.when(step == pl.num_programs(0) - 1)
    def finish():
        radix = 8
        other = tiles // radix
        columns = radix // 2 + 1

        def one_spectrum(s, carry):
            base = s * tiles * SUB
            present = {}
            for b in range(other):
                got = [
                    (w_ref[pl.ds(pl.multiple_of(base + (other * a + b) * SUB, SUB), SUB), :], None)
                    for a in range(radix)
                ]
                for ka, (re, im) in enumerate(fft(got, columns)):
                    if ka:
                        re, im = turn(re, im, ka * b, tiles)
                    for c, value in enumerate((re, im)):
                        present[ka, b, c] = value is not None
                        if value is not None:
                            at = ((ka * other + b) * 2 + c) * SUB
                            a_ref[at : at + SUB, :] = value
            for ka in range(columns):
                got = []
                for b in range(other):
                    at = (ka * other + b) * 2 * SUB
                    got.append(
                        tuple(
                            a_ref[at + c * SUB : at + (c + 1) * SUB, :] if present[ka, b, c] else None
                            for c in range(2)
                        )
                    )
                need = other if 0 < ka else other // 2 + 1
                done = fft(got, need)
                for kb, (re, im) in enumerate(done):
                    direct = ka + radix * kb
                    if direct <= half:
                        k1, conj = direct, False
                    else:
                        k1, conj = tiles - direct, True
                        if k1 % radix == ka:
                            continue
                    if im is None:
                        im = jnp.zeros_like(re)
                    if conj:
                        im = -im
                    cos = tw_ref[k1 * 2 * SUB : (k1 * 2 + 1) * SUB, :]
                    sin = tw_ref[(k1 * 2 + 1) * SUB : (k1 * 2 + 2) * SUB, :]
                    where = k1 * spectra_count + s
                    f_ref[pl.ds(where, SUB, stride=pitch), :] = re * cos + im * sin
                    f_ref[pl.ds(SUB * pitch + where, SUB, stride=pitch), :] = im * cos - re * sin
            return carry

        lax.fori_loop(0, spectra_count, one_spectrum, 0)

        def one_input(one, carry):
            for c in range(2):
                value = f_ref[pl.ds((c * SUB + one) * pitch, rows), :]
                high = value.astype(bf16)
                xp_ref[:, c * LANES : (c + 1) * LANES] = high
                xp_ref[:, (2 + c) * LANES : (3 + c) * LANES] = (value - high.astype(f32)).astype(bf16)
            for j in range(parts):
                if j < parts // 2:
                    first = j * block
                    which = 0
                else:
                    first = ((parts - 1 - j) * AVG + 1) * spectra_count
                    which = 1
                high = xp_ref[first : first + block, : 2 * LANES]
                low = xp_ref[first : first + block, 2 * LANES :]
                dims = (((1,), (1,)), ((), ()))
                both = lax.dot_general(t_ref[which], high, dims, preferred_element_type=f32)
                more = lax.dot_general(t_ref[which, : 2 * kept], low, dims, preferred_element_type=f32)
                out = both[: 2 * kept] + (both[2 * kept :] + more)
                for c in range(2):
                    for h in range(block // LANES):
                        tile = (j * 2 + c) * (block // LANES) + h
                        s_ref[pl.ds(tile * kept * SKEW + one, kept, stride=SKEW), :] = out[
                            c * kept : (c + 1) * kept, h * LANES : (h + 1) * LANES
                        ]
            return carry

        lax.fori_loop(0, inputs, one_input, 0)

        wide = 2 * block // LANES
        near = math.gcd(kept // chans, 2)

        def staged(m):
            for j in range(parts):
                for tile in range(wide):
                    z_ref[m * parts + j, :, tile * LANES : (tile + 1) * LANES] = s_ref[
                        pl.ds(((j * wide + tile) * kept + m) * SKEW, inputs), :
                    ].astype(bf16)

        copies = []
        for dc in range(chans):
            chan = lax.rem(lax.axis_index("chan") + dc, chans) if turned else dc

            def some_rows(at, carry, chan=chan):
                for one in range(near):
                    staged(chan * (kept // chans) + at * near + one)
                return carry

            lax.fori_loop(0, kept // chans // near, some_rows, 0)
            for index, (dz, of, skip, count) in enumerate(sends):
                if of != dc:
                    continue
                first = chan * (kept // chans * parts) + skip
                if dz is not None:
                    station = lax.rem(lax.axis_index("stn") + dz, stations)
                    first = first + station * (kept // chans * parts // stations)
                copies.append(
                    pltpu.make_async_copy(z_ref.at[pl.ds(first, count)], outs[index], sems.at[index])
                )
                copies[-1].start()
        for copy in copies:
            copy.wait()


def tables(frame_len):
    tiles = frame_len // LANES
    half = tiles // 2
    kept = LANES // 2
    k1 = np.arange(half + 1)[:, None]
    p = np.arange(LANES)[None, :]
    angle = 2 * np.pi * ((k1 * p) % frame_len) / frame_len
    tw = np.stack([np.cos(angle), np.sin(angle)], axis=1)[:, :, None, :]
    tw = np.broadcast_to(tw, (half + 1, 2, SUB, LANES)).reshape(-1, LANES).astype(np.float32)

    def one(m, sign):
        theta = 2 * np.pi * ((m[:, None] * p) % LANES) / LANES
        cos, sin = np.cos(theta), np.sin(theta)
        full = np.concatenate(
            [np.concatenate([cos, sin], axis=1), sign * np.concatenate([-sin, cos], axis=1)], axis=0
        )
        full = (full * frame_len ** (-0.5)).astype(np.float32)
        high = full.astype(jnp.bfloat16)
        low = (full - high.astype(np.float32)).astype(jnp.bfloat16)
        return np.concatenate([high, low], axis=0)

    m = np.arange(kept)
    return tw, np.stack([one(m, 1.0), one(LANES - 1 - m, -1.0)])


HBM = pl.BlockSpec(memory_space=pl.ANY)


def make_spectra(voltages, taps, sends, stations, chans, turned):
    frames, inputs, frame_len = voltages.shape
    tap_count = taps.shape[0]
    spectra_count = frames - tap_count + 1
    tiles = frame_len // LANES
    half = tiles // 2
    rows = (half + 1) * spectra_count
    block = AVG * spectra_count
    groups = frame_len // 2 // AVG
    per_step = 8
    tw, t = tables(frame_len)
    sizes = (inputs, frames, tiles, per_step, spectra_count, tap_count, stations, chans)
    return pl.pallas_call(
        functools.partial(spectra_kernel, sizes=sizes, sends=sends, turned=turned),
        name="spectra",
        grid=(tiles // per_step,),
        in_specs=[
            pl.BlockSpec(tw.shape, lambda q: (0, 0)),
            pl.BlockSpec(t.shape, lambda q: (0, 0, 0)),
            pl.BlockSpec((frames, inputs, per_step * LANES), lambda q: (0, 0, q)),
            pl.BlockSpec((tap_count, per_step * LANES), lambda q: (0, q)),
        ],
        out_specs=[HBM] * len(sends),
        out_shape=[jax.ShapeDtypeStruct((count, inputs, 2 * block), bf16) for _, _, _, count in sends],
        scratch_shapes=[
            pltpu.VMEM((spectra_count * tiles * SUB, LANES), f32),
            pltpu.VMEM((5 * (tiles // 8) * 2 * SUB, LANES), f32),
            pltpu.VMEM((2 * SUB * (rows + 4), LANES), f32),
            pltpu.VMEM((rows, 4 * LANES), bf16),
            pltpu.VMEM((groups * (2 * block // LANES) * SKEW, LANES), f32),
            pltpu.VMEM((groups, inputs, 2 * block), bf16),
            pltpu.SemaphoreType.DMA((len(sends),)),
        ],
    )(jnp.asarray(tw), jnp.asarray(t), voltages, taps)


def lefts(own):
    wide = own.shape[1]
    return [own, jnp.concatenate([own[:, wide // 2 :], -own[:, : wide // 2]], axis=1)]


def tiles_of(blocks, slot, p_ref, q_ref, scale):
    target, rest = blocks
    block_inputs = target.shape[0]
    copies = LANES // block_inputs
    out_rows = block_inputs * block_inputs // LANES
    place = lax.broadcasted_iota(jnp.int32, (out_rows, LANES), 1) // block_inputs
    right = jnp.concatenate([target] * copies, axis=0)
    left = jnp.concatenate([piece for pair in rest for piece in pair], axis=0)
    out = lax.dot_general(left, right, (((1,), (1,)), ((), ())), preferred_element_type=f32)
    p_ref[slot, :, :] = out * scale
    tiles = []
    for d in range(len(rest)):
        for part in range(2):
            base = (2 * d + part) * block_inputs
            value = p_ref[slot, pl.ds(base, out_rows, stride=copies), :]
            for r in range(1, copies):
                value = jnp.where(place == r, p_ref[slot, pl.ds(base + r, out_rows, stride=copies), :], value)
            q_ref[slot, d, pl.ds(part, out_rows, stride=2), :] = value
        tiles.append(q_ref[slot, d].astype(bf16))
    return tiles


def correlate_kernel(r_ref, o_ref, p_ref, q_ref, *, sizes):
    stations, chans, reach, scale = sizes

    def one_target(target, carry):
        owns = []
        for d in range(reach):
            b = lax.rem(target - d + stations, stations)
            owns.append(jnp.concatenate([r_ref[c * stations + b, 0] for c in range(chans)], axis=0))
        tiles = tiles_of((owns[0], [lefts(own) for own in owns]), 0, p_ref, q_ref, scale)
        for d, tile in enumerate(tiles):
            o_ref[lax.rem(target - d + stations, stations), d, 0, :, :] = tile
        return carry

    lax.fori_loop(0, stations, one_target, 0)


def correlate(turned, stations, chans, reach, scale):
    sources, groups, inputs, wide = turned.shape
    block_inputs = chans * inputs
    out_rows = block_inputs * block_inputs // LANES
    return pl.pallas_call(
        functools.partial(correlate_kernel, sizes=(stations, chans, reach, scale)),
        name="correlate",
        grid=(groups,),
        in_specs=[pl.BlockSpec((sources, 1, inputs, wide), lambda g: (0, g, 0, 0))],
        out_specs=pl.BlockSpec((stations, reach, 1, 2 * out_rows, LANES), lambda g: (0, 0, g, 0, 0)),
        out_shape=jax.ShapeDtypeStruct((stations, reach, groups, 2 * out_rows, LANES), bf16),
        scratch_shapes=[
            pltpu.VMEM((1, reach * 2 * block_inputs, LANES), f32),
            pltpu.VMEM((1, reach, 2 * out_rows, LANES), f32),
        ],
    )(turned)


def pieces_kernel(*refs, sizes, pieces):
    blocks, chans, groups, distances, scale, per_step = sizes
    arrived = refs[: len(pieces)]
    outs = refs[len(pieces) : len(pieces) + blocks]
    r_ref, p_ref, q_ref, sems = refs[len(pieces) + blocks :]
    copies = []
    for index, (block, dc, mine, first) in enumerate(pieces):
        chan = lax.rem(lax.axis_index("chan") - dc + chans, chans)
        start = first + lax.axis_index("stn") * mine if mine else first
        copies.append(
            pltpu.make_async_copy(
                arrived[index].at[pl.ds(start, groups)], r_ref.at[block * chans + chan], sems.at[index]
            )
        )
        copies[-1].start()
    for copy in copies:
        copy.wait()

    def some_groups(at, carry):
        for one in range(per_step):
            g = at * per_step + one
            owns = [
                jnp.concatenate([r_ref[block * chans + c, g] for c in range(chans)], axis=0)
                for block in range(blocks)
            ]
            pairs = [lefts(own) for own in owns]
            for target in range(blocks):
                who = [(target - d) % blocks for d in distances]
                tiles = tiles_of(
                    (owns[target], [pairs[b] for b in who]), one * blocks + target, p_ref, q_ref, scale
                )
                for d, (b, tile) in enumerate(zip(who, tiles)):
                    outs[b][d, g, :, :] = tile
        return carry

    lax.fori_loop(0, groups // per_step, some_groups, 0)


def correlate_pieces(arrays, pieces, blocks, chans, groups, distances, scale, stays):
    inputs, wide = arrays[0].shape[1:]
    block_inputs = chans * inputs
    out_rows = block_inputs * block_inputs // LANES
    per_step = math.gcd(groups, 8 // blocks)
    sizes = (blocks, chans, groups, distances, scale, per_step)
    shape = (len(distances), groups, 2 * out_rows, LANES)
    vmem = pl.BlockSpec(memory_space=pltpu.VMEM)
    return pl.pallas_call(
        functools.partial(pieces_kernel, sizes=sizes, pieces=pieces),
        in_specs=[HBM if local else vmem for local in stays],
        out_specs=[vmem] * blocks,
        out_shape=[jax.ShapeDtypeStruct(shape, bf16)] * blocks,
        scratch_shapes=[
            pltpu.VMEM((blocks * chans, groups, inputs, wide), bf16),
            pltpu.VMEM((per_step * blocks, len(distances) * 2 * block_inputs, LANES), f32),
            pltpu.VMEM((per_step * blocks, len(distances), 2 * out_rows, LANES), f32),
            pltpu.SemaphoreType.DMA((len(pieces),)),
        ],
    )(*arrays)


def assemble_kernel(own_ref, *refs, stations, chunks):
    parts = refs[:-1]
    out_ref = refs[-1]
    out_ref[0, :, :, :] = own_ref[0]
    for dz in range(stations):
        host = lax.rem(lax.axis_index("stn") - dz + stations, stations)
        for chunk in range(chunks):
            part = parts[dz * chunks + chunk]
            count = part.shape[1]
            at = (host * chunks + chunk) * count
            for d in range(part.shape[0]):
                out_ref[d + 1, pl.ds(at, count), :, :] = part[d]


def assemble(own, parts, stations, chunks):
    reach = parts[0].shape[0] + 1
    vmem = pl.BlockSpec(memory_space=pltpu.VMEM)
    return pl.pallas_call(
        functools.partial(assemble_kernel, stations=stations, chunks=chunks),
        name="assemble",
        in_specs=[vmem] * (1 + len(parts)),
        out_specs=vmem,
        out_shape=jax.ShapeDtypeStruct((reach,) + own.shape[1:], bf16),
    )(own, *parts)


def shifted(value, stations, chans, dz, dc):
    pairs = [
        (z * chans + c, (z + dz) % stations * chans + (c + dc) % chans)
        for z in range(stations)
        for c in range(chans)
    ]
    return lax.ppermute(value, ("stn", "chan"), pairs)


def local(voltages, taps):
    inputs_here, frames, frame_len = voltages.shape
    spectra_count = frames - taps.shape[0] + 1
    stations = lax.axis_size("stn")
    chans = lax.axis_size("chan")
    reach = stations // 2 + 1
    block_inputs = chans * inputs_here
    pairs = block_inputs * block_inputs
    groups = frame_len // 2 // AVG
    here = groups // (stations * chans)
    scale = 1.0 / (spectra_count * AVG)
    frames_first = voltages.transpose(1, 0, 2)
    if not direct(stations, chans):
        sends = tuple((None, dc, 0, groups // chans) for dc in range(chans))
        slices = make_spectra(frames_first, taps, sends, stations, chans, False)
        send = jnp.concatenate(slices, axis=0).reshape(chans * stations, here, inputs_here, -1)
        turned = lax.all_to_all(send, ("chan", "stn"), 0, 0, tiled=True)
        tiles = correlate(turned, stations, chans, reach, scale)
        back = lax.all_to_all(tiles, "stn", 0, 0, tiled=True)
        out = back.transpose(1, 0, 2, 3, 4)
    else:
        part = here // CHUNKS
        sends = [(None, dc, 0, here * stations) for dc in range(chans)]
        for chunk in range(CHUNKS):
            sends += [(dz, dc, chunk * part, part) for dz in (2, 1, 3)[: stations - 1] for dc in range(chans)]
        sent = make_spectra(frames_first, taps, tuple(sends), stations, chans, True)
        whole, got = [], {}
        for (dz, dc, skip, _), value in zip(sends, sent):
            if dz is None:
                whole.append(shifted(value, stations, chans, 0, dc) if dc else value)
            else:
                got[dz, dc, skip // part] = shifted(value, stations, chans, dz, dc)
        stays = [dc == 0 for dc in range(chans)]
        pieces = [(0, dc, 0, 0) for dc in range(chans)]
        (own,) = correlate_pieces(whole, pieces, 1, chans, here * stations, (0,), scale, stays)
        distances = tuple(range(1, reach))
        back = {}
        for chunk in range(CHUNKS):
            pieces = [(0, dc, here, chunk * part) for dc in range(chans)]
            arrays = list(whole)
            for dz in range(1, stations):
                for dc in range(chans):
                    pieces.append((-dz % stations, dc, 0, 0))
                    arrays.append(got[dz, dc, chunk])
            outs = correlate_pieces(
                arrays, pieces, stations, chans, part, distances, scale, stays + [False] * (len(arrays) - chans)
            )
            for dz in range(stations):
                back[dz, chunk] = outs[0] if dz == 0 else shifted(outs[dz], stations, chans, dz, 0)
        out = assemble(
            own, [back[dz, chunk] for dz in range(stations) for chunk in range(CHUNKS)], stations, CHUNKS
        )
    out = out.reshape(reach, stations * here, pairs // LANES, 2, LANES)
    return out.transpose(0, 1, 3, 2, 4).reshape(1, reach, stations * here, 2, pairs)


CHUNKS = 2


def direct(stations, chans):
    return 2 < stations <= 4 and stations * chans <= 16


def solution(mesh):
    placed = (P(("grp", "stn", "chan"), None, None), P())

    return jax.shard_map(
        local,
        mesh=mesh,
        in_specs=placed,
        out_specs=P(("grp", "stn"), None, "chan", None, None),
        check_vma=False,
    )
```

```python
import functools
import math

import jax
import jax.numpy as jnp
import numpy as np
from jax import lax
from jax.experimental import pallas as pl
from jax.experimental.pallas import tpu as pltpu
from jax.sharding import PartitionSpec as P


AVG = 16
LANES = 128
SUB = 8
f32 = jnp.float32
bf16 = jnp.bfloat16


def add(a, b):
    return b if a is None else a if b is None else a + b


def sub(a, b):
    if b is None:
        return a
    return -b if a is None else a - b


def turn(re, im, num, den):
    num %= den
    if num == 0:
        return re, im
    if 4 * num == den:
        return im, None if re is None else -re
    if 2 * num == den:
        return (None if re is None else -re), (None if im is None else -im)
    if 4 * num == 3 * den:
        return (None if im is None else -im), re
    c = math.cos(2 * math.pi * num / den)
    s = math.sin(2 * math.pi * num / den)
    if 8 * num == den or 8 * num == 5 * den:
        if im is None:
            return re * c, re * -s
        if re is None:
            return im * s, im * c
        return (re + im) * c, (im - re) * c
    if im is None:
        return re * c, re * -s
    if re is None:
        return im * s, im * c
    return re * c + im * s, im * c - re * s


def fft(values, needed):
    size = len(values)
    if size == 1:
        return values
    if all(im is None for _, im in values):
        half_need = size // 4 + 1 if size >= 4 else size // 2
        even = fft(values[0::2], min(half_need, size // 2))
        odd = fft(values[1::2], min(half_need, size // 2))

        def mirrored(part, k):
            n = size // 2
            if k < len(part):
                return part[k]
            re, im = part[n - k]
            return re, (None if im is None else -im)

        out = [None] * size
        for k in range(size // 2):
            if k >= needed and k + size // 2 >= needed:
                continue
            er, ei = mirrored(even, k)
            tr, ti = turn(*mirrored(odd, k), k, size)
            out[k] = (add(er, tr), add(ei, ti))
            out[k + size // 2] = (sub(er, tr), sub(ei, ti))
        return out[:needed]
    even = fft(values[0::2], size // 2)
    odd = fft(values[1::2], size // 2)
    out = [None] * size
    for k in range(size // 2):
        er, ei = even[k]
        tr, ti = turn(*odd[k], k, size)
        out[k] = (add(er, tr), add(ei, ti))
        out[k + size // 2] = (sub(er, tr), sub(ei, ti))
    return out[:needed]


def filtered(x, weights, spectra_count):
    tap_count = len(weights)

    def correlated(h, v, count):
        out = []
        for n in range(count):
            total = h[0] * v[n]
            for k in range(1, len(h)):
                total = total + h[k] * v[n + k]
            out.append(total)
        return out

    if tap_count % 2 or spectra_count % 2:
        return correlated(weights, x, spectra_count)
    even, odd = weights[0::2], weights[1::2]
    first, second = x[0::2], x[1::2]
    count = spectra_count // 2
    need = count + tap_count // 2 - 1
    shared = correlated([e + o for e, o in zip(even, odd)], second, count)
    left = correlated(even, [first[n] - second[n] for n in range(need)], count)
    right = correlated(odd, [first[n + 1] - second[n] for n in range(need)], count)
    out = []
    for n in range(count):
        out += [shared[n] + left[n], shared[n] + right[n]]
    return out


SKEW = SUB + 1


def spectra_kernel(tw_ref, t_ref, x_ref, taps_ref, *refs, sizes, sends, turned):
    inputs, frames, tiles, per_step, spectra_count, tap_count, stations, chans = sizes
    outs = refs[: len(sends)]
    w_ref, a_ref, f_ref, xp_ref, s_ref, z_ref, sems = refs[len(sends) :]
    half = tiles // 2
    kept = LANES // 2
    rows = (half + 1) * spectra_count
    pitch = rows + 4
    block = AVG * spectra_count
    parts = tiles // AVG
    step = pl.program_id(0)

    def one_tile(here, carry):
        lanes = pl.ds(pl.multiple_of(here * LANES, LANES), LANES)
        x = [x_ref[frame, :, lanes].astype(f32) for frame in range(frames)]
        weights = [jnp.broadcast_to(taps_ref[t : t + 1, lanes], (inputs, LANES)) for t in range(tap_count)]
        at = (step * per_step + here) * SUB
        for s, total in enumerate(filtered(x, weights, spectra_count)):
            w_ref[pl.ds(pl.multiple_of(s * tiles * SUB + at, SUB), inputs), :] = total
        return carry

    lax.fori_loop(0, per_step, one_tile, 0)

    @pl.when(step == pl.num_programs(0) - 1)
    def finish():
        radix = 8
        other = tiles // radix
        columns = radix // 2 + 1

        def one_spectrum(s, carry):
            base = s * tiles * SUB
            present = {}
            for b in range(other):
                got = [
                    (w_ref[pl.ds(pl.multiple_of(base + (other * a + b) * SUB, SUB), SUB), :], None)
                    for a in range(radix)
                ]
                for ka, (re, im) in enumerate(fft(got, columns)):
                    if ka:
                        re, im = turn(re, im, ka * b, tiles)
                    for c, value in enumerate((re, im)):
                        present[ka, b, c] = value is not None
                        if value is not None:
                            at = ((ka * other + b) * 2 + c) * SUB
                            a_ref[at : at + SUB, :] = value
            for ka in range(columns):
                got = []
                for b in range(other):
                    at = (ka * other + b) * 2 * SUB
                    got.append(
                        tuple(
                            a_ref[at + c * SUB : at + (c + 1) * SUB, :] if present[ka, b, c] else None
                            for c in range(2)
                        )
                    )
                need = other if 0 < ka else other // 2 + 1
                done = fft(got, need)
                for kb, (re, im) in enumerate(done):
                    direct = ka + radix * kb
                    if direct <= half:
                        k1, conj = direct, False
                    else:
                        k1, conj = tiles - direct, True
                        if k1 % radix == ka:
                            continue
                    if im is None:
                        im = jnp.zeros_like(re)
                    if conj:
                        im = -im
                    cos = tw_ref[k1 * 2 * SUB : (k1 * 2 + 1) * SUB, :]
                    sin = tw_ref[(k1 * 2 + 1) * SUB : (k1 * 2 + 2) * SUB, :]
                    where = k1 * spectra_count + s
                    f_ref[pl.ds(where, SUB, stride=pitch), :] = re * cos + im * sin
                    f_ref[pl.ds(SUB * pitch + where, SUB, stride=pitch), :] = im * cos - re * sin
            return carry

        lax.fori_loop(0, spectra_count, one_spectrum, 0)

        def one_input(one, carry):
            for c in range(2):
                value = f_ref[pl.ds((c * SUB + one) * pitch, rows), :]
                high = value.astype(bf16)
                xp_ref[:, c * LANES : (c + 1) * LANES] = high
                xp_ref[:, (2 + c) * LANES : (3 + c) * LANES] = (value - high.astype(f32)).astype(bf16)
            for j in range(parts):
                if j < parts // 2:
                    first = j * block
                    which = 0
                else:
                    first = ((parts - 1 - j) * AVG + 1) * spectra_count
                    which = 1
                high = xp_ref[first : first + block, : 2 * LANES]
                low = xp_ref[first : first + block, 2 * LANES :]
                dims = (((1,), (1,)), ((), ()))
                both = lax.dot_general(t_ref[which], high, dims, preferred_element_type=f32)
                more = lax.dot_general(t_ref[which, : 2 * kept], low, dims, preferred_element_type=f32)
                out = both[: 2 * kept] + (both[2 * kept :] + more)
                for c in range(2):
                    for h in range(block // LANES):
                        tile = (j * 2 + c) * (block // LANES) + h
                        s_ref[pl.ds(tile * kept * SKEW + one, kept, stride=SKEW), :] = out[
                            c * kept : (c + 1) * kept, h * LANES : (h + 1) * LANES
                        ]
            return carry

        lax.fori_loop(0, inputs, one_input, 0)

        wide = 2 * block // LANES
        near = math.gcd(kept // chans, 2)

        def staged(m):
            for j in range(parts):
                for tile in range(wide):
                    z_ref[m * parts + j, :, tile * LANES : (tile + 1) * LANES] = s_ref[
                        pl.ds(((j * wide + tile) * kept + m) * SKEW, inputs), :
                    ].astype(bf16)

        copies = []
        for dc in range(chans):
            chan = lax.bitwise_xor(lax.axis_index("chan"), dc) if turned else dc

            def some_rows(at, carry, chan=chan):
                for one in range(near):
                    staged(chan * (kept // chans) + at * near + one)
                return carry

            lax.fori_loop(0, kept // chans // near, some_rows, 0)
            for index, (dz, of, skip, count) in enumerate(sends):
                if of != dc:
                    continue
                first = chan * (kept // chans * parts) + skip
                if dz is not None:
                    station = lax.bitwise_xor(lax.axis_index("stn"), dz)
                    first = first + station * (kept // chans * parts // stations)
                copies.append(
                    pltpu.make_async_copy(z_ref.at[pl.ds(first, count)], outs[index], sems.at[index])
                )
                copies[-1].start()
        for copy in copies:
            copy.wait()


def tables(frame_len):
    tiles = frame_len // LANES
    half = tiles // 2
    kept = LANES // 2
    k1 = np.arange(half + 1)[:, None]
    p = np.arange(LANES)[None, :]
    angle = 2 * np.pi * ((k1 * p) % frame_len) / frame_len
    tw = np.stack([np.cos(angle), np.sin(angle)], axis=1)[:, :, None, :]
    tw = np.broadcast_to(tw, (half + 1, 2, SUB, LANES)).reshape(-1, LANES).astype(np.float32)

    def one(m, sign):
        theta = 2 * np.pi * ((m[:, None] * p) % LANES) / LANES
        cos, sin = np.cos(theta), np.sin(theta)
        full = np.concatenate(
            [np.concatenate([cos, sin], axis=1), sign * np.concatenate([-sin, cos], axis=1)], axis=0
        )
        full = (full * frame_len ** (-0.5)).astype(np.float32)
        high = full.astype(jnp.bfloat16)
        low = (full - high.astype(np.float32)).astype(jnp.bfloat16)
        return np.concatenate([high, low], axis=0)

    m = np.arange(kept)
    return tw, np.stack([one(m, 1.0), one(LANES - 1 - m, -1.0)])


HBM = pl.BlockSpec(memory_space=pl.ANY)


def make_spectra(voltages, taps, sends, stations, chans, turned):
    frames, inputs, frame_len = voltages.shape
    tap_count = taps.shape[0]
    spectra_count = frames - tap_count + 1
    tiles = frame_len // LANES
    half = tiles // 2
    rows = (half + 1) * spectra_count
    block = AVG * spectra_count
    groups = frame_len // 2 // AVG
    per_step = 8
    tw, t = tables(frame_len)
    sizes = (inputs, frames, tiles, per_step, spectra_count, tap_count, stations, chans)
    return pl.pallas_call(
        functools.partial(spectra_kernel, sizes=sizes, sends=sends, turned=turned),
        name="spectra",
        grid=(tiles // per_step,),
        in_specs=[
            pl.BlockSpec(tw.shape, lambda q: (0, 0)),
            pl.BlockSpec(t.shape, lambda q: (0, 0, 0)),
            pl.BlockSpec((frames, inputs, per_step * LANES), lambda q: (0, 0, q)),
            pl.BlockSpec((tap_count, per_step * LANES), lambda q: (0, q)),
        ],
        out_specs=[HBM] * len(sends),
        out_shape=[jax.ShapeDtypeStruct((count, inputs, 2 * block), bf16) for _, _, _, count in sends],
        scratch_shapes=[
            pltpu.VMEM((spectra_count * tiles * SUB, LANES), f32),
            pltpu.VMEM((5 * (tiles // 8) * 2 * SUB, LANES), f32),
            pltpu.VMEM((2 * SUB * (rows + 4), LANES), f32),
            pltpu.VMEM((rows, 4 * LANES), bf16),
            pltpu.VMEM((groups * (2 * block // LANES) * SKEW, LANES), f32),
            pltpu.VMEM((groups, inputs, 2 * block), bf16),
            pltpu.SemaphoreType.DMA((len(sends),)),
        ],
    )(jnp.asarray(tw), jnp.asarray(t), voltages, taps)


def lefts(own):
    wide = own.shape[1]
    return [own, jnp.concatenate([own[:, wide // 2 :], -own[:, : wide // 2]], axis=1)]


def products(p_ref, slot, owns):
    right = jnp.concatenate(owns, axis=0)
    left = jnp.concatenate([piece for own in owns for piece in lefts(own)], axis=0)
    out = lax.dot_general(left, right, (((1,), (1,)), ((), ())), preferred_element_type=f32)
    p_ref[slot, :, : right.shape[0]] = out


def tiles_of(p_ref, q_ref, slot, at, block, targets, block_inputs, scale):
    copies = LANES // block_inputs
    out_rows = block_inputs * block_inputs // LANES
    place = lax.broadcasted_iota(jnp.int32, (out_rows, LANES), 1) // block_inputs
    for part in range(2):
        base = (2 * block + part) * block_inputs
        rows = [p_ref[slot, pl.ds(base + r, out_rows, stride=copies), :] for r in range(copies)]
        for index, target in enumerate(targets):
            value = None
            for r in range(copies):
                shift = (r - target) % copies if isinstance(target, int) else lax.rem(r - target + copies, copies)
                moved = rows[r]
                if not (isinstance(shift, int) and shift == 0):
                    moved = pltpu.roll(moved, shift * block_inputs, 1)
                value = moved if r == 0 else jnp.where(place == r, moved, value)
            q_ref[at + index, pl.ds(part, out_rows, stride=2), :] = value * scale
    return [q_ref[at + index].astype(bf16) for index in range(len(targets))]


def correlate_kernel(r_ref, o_ref, p_ref, q_ref, *, sizes):
    stations, chans, reach, scale = sizes

    block_inputs = chans * r_ref.shape[2]

    def one_block(b, carry):
        def fetch(block):
            return jnp.concatenate([r_ref[c * stations + block, 0] for c in range(chans)], axis=0)

        own = fetch(b)
        for d in range(reach):
            other = lax.rem(b + d, stations)
            right = fetch(other)
            left = jnp.concatenate(lefts(own), axis=0)
            p_ref[d, :, :block_inputs] = lax.dot_general(
                left, right, (((1,), (1,)), ((), ())), preferred_element_type=f32
            )
            (tile,) = tiles_of(p_ref, q_ref, d, d, 0, [0], block_inputs, scale)
            o_ref[b, d, 0, :, :] = tile
        return carry

    lax.fori_loop(0, stations, one_block, 0)


def correlate(turned, stations, chans, reach, scale):
    sources, groups, inputs, wide = turned.shape
    block_inputs = chans * inputs
    out_rows = block_inputs * block_inputs // LANES
    return pl.pallas_call(
        functools.partial(correlate_kernel, sizes=(stations, chans, reach, scale)),
        name="correlate",
        grid=(groups,),
        in_specs=[pl.BlockSpec((sources, 1, inputs, wide), lambda g: (0, g, 0, 0))],
        out_specs=pl.BlockSpec((stations, reach, 1, 2 * out_rows, LANES), lambda g: (0, 0, g, 0, 0)),
        out_shape=jax.ShapeDtypeStruct((stations, reach, groups, 2 * out_rows, LANES), bf16),
        scratch_shapes=[
            pltpu.VMEM((reach, 2 * block_inputs, LANES), f32),
            pltpu.VMEM((reach, 2 * out_rows, LANES), f32),
        ],
    )(turned)


def pieces_kernel(*refs, sizes, pieces):
    blocks, chans, groups, distances, scale, per_step = sizes
    arrived = refs[: len(pieces)]
    outs = refs[len(pieces) : len(pieces) + blocks]
    r_ref, p_ref, q_ref, sems = refs[len(pieces) + blocks :]
    here = lax.axis_index("stn") if blocks > 1 else 0
    block_inputs = chans * r_ref.shape[2]
    copies = []
    for index, (dz, dc, mine, first) in enumerate(pieces):
        chan = lax.bitwise_xor(lax.axis_index("chan"), dc)
        block = lax.bitwise_xor(here, dz) if blocks > 1 else 0
        start = first + lax.axis_index("stn") * mine if mine else first
        copies.append(
            pltpu.make_async_copy(
                arrived[index].at[pl.ds(start, groups)], r_ref.at[block * chans + chan], sems.at[index]
            )
        )
        copies[-1].start()
    for copy in copies:
        copy.wait()

    def some_groups(at, carry):
        for one in range(per_step):
            g = at * per_step + one
            owns = [
                jnp.concatenate([r_ref[block * chans + c, g] for c in range(chans)], axis=0)
                for block in range(blocks)
            ]
            products(p_ref, one, owns)
            for turn_by in range(blocks):
                block = lax.bitwise_xor(here, turn_by) if blocks > 1 else 0
                targets = [lax.rem(block + d, blocks) if blocks > 1 else 0 for d in distances]
                first = (one * blocks + turn_by) * len(distances)
                tiles = tiles_of(p_ref, q_ref, one, first, block, targets, block_inputs, scale)
                for d, tile in enumerate(tiles):
                    outs[turn_by][d, g, :, :] = tile
        return carry

    lax.fori_loop(0, groups // per_step, some_groups, 0)


def correlate_pieces(arrays, pieces, blocks, chans, groups, distances, scale, stays):
    inputs, wide = arrays[0].shape[1:]
    block_inputs = chans * inputs
    out_rows = block_inputs * block_inputs // LANES
    per_step = math.gcd(groups, 8 // blocks)
    sizes = (blocks, chans, groups, distances, scale, per_step)
    shape = (len(distances), groups, 2 * out_rows, LANES)
    vmem = pl.BlockSpec(memory_space=pltpu.VMEM)
    return pl.pallas_call(
        functools.partial(pieces_kernel, sizes=sizes, pieces=pieces),
        in_specs=[HBM if local else vmem for local in stays],
        out_specs=[vmem] * blocks,
        out_shape=[jax.ShapeDtypeStruct(shape, bf16)] * blocks,
        scratch_shapes=[
            pltpu.VMEM((blocks * chans, groups, inputs, wide), bf16),
            pltpu.VMEM((per_step, blocks * 2 * block_inputs, LANES), f32),
            pltpu.VMEM((per_step * blocks * len(distances), 2 * out_rows, LANES), f32),
            pltpu.SemaphoreType.DMA((len(pieces),)),
        ],
    )(*arrays)


def assemble_kernel(own_ref, *refs, stations, chunks):
    parts = refs[:-1]
    out_ref = refs[-1]
    out_ref[0, :, :, :] = own_ref[0]
    for dz in range(stations):
        host = lax.bitwise_xor(lax.axis_index("stn"), dz)
        for chunk in range(chunks):
            part = parts[dz * chunks + chunk]
            count = part.shape[1]
            at = (host * chunks + chunk) * count
            for d in range(part.shape[0]):
                out_ref[d + 1, pl.ds(at, count), :, :] = part[d]


def assemble(own, parts, stations, chunks):
    reach = parts[0].shape[0] + 1
    vmem = pl.BlockSpec(memory_space=pltpu.VMEM)
    return pl.pallas_call(
        functools.partial(assemble_kernel, stations=stations, chunks=chunks),
        name="assemble",
        in_specs=[vmem] * (1 + len(parts)),
        out_specs=vmem,
        out_shape=jax.ShapeDtypeStruct((reach,) + own.shape[1:], bf16),
    )(own, *parts)


def shifted(value, stations, chans, dz, dc):
    pairs = [
        (z * chans + c, (z ^ dz) * chans + (c ^ dc))
        for z in range(stations)
        for c in range(chans)
    ]
    return lax.ppermute(value, ("stn", "chan"), pairs)


def local(voltages, taps):
    inputs_here, frames, frame_len = voltages.shape
    spectra_count = frames - taps.shape[0] + 1
    stations = lax.axis_size("stn")
    chans = lax.axis_size("chan")
    reach = stations // 2 + 1
    block_inputs = chans * inputs_here
    pairs = block_inputs * block_inputs
    groups = frame_len // 2 // AVG
    here = groups // (stations * chans)
    scale = 1.0 / (spectra_count * AVG)
    frames_first = voltages.transpose(1, 0, 2)
    if not direct(stations, chans):
        sends = tuple((None, dc, 0, groups // chans) for dc in range(chans))
        slices = make_spectra(frames_first, taps, sends, stations, chans, False)
        send = jnp.concatenate(slices, axis=0).reshape(chans * stations, here, inputs_here, -1)
        turned = lax.all_to_all(send, ("chan", "stn"), 0, 0, tiled=True)
        tiles = correlate(turned, stations, chans, reach, scale)
        back = lax.all_to_all(tiles, "stn", 0, 0, tiled=True)
        out = back.transpose(1, 0, 2, 3, 4)
    else:
        part = here // CHUNKS
        sends = [(None, dc, 0, here * stations) for dc in range(chans)]
        sends += [(dz, dc, 0, here) for dz in (2, 1, 3) for dc in range(chans)]
        sent = make_spectra(frames_first, taps, tuple(sends), stations, chans, True)
        whole, far = [], {}
        for (dz, dc, _, _), value in zip(sends, sent):
            if dz is None:
                whole.append(shifted(value, stations, chans, 0, dc) if dc else value)
            else:
                far[dz, dc] = shifted(value, stations, chans, dz, dc)
        stays = [dc == 0 for dc in range(chans)]
        pieces = [(0, dc, 0, 0) for dc in range(chans)]
        (own,) = correlate_pieces(whole, pieces, 1, chans, here * stations, (0,), scale, stays)
        distances = tuple(range(1, reach))
        back = {}
        for chunk in range(CHUNKS):
            pieces = [(0, dc, here, chunk * part) for dc in range(chans)]
            pieces += [(dz, dc, 0, chunk * part) for dz, dc in far]
            arrays = whole + list(far.values())
            inside = stays + [False] * len(far)
            outs = correlate_pieces(arrays, pieces, stations, chans, part, distances, scale, inside)
            for dz in range(stations):
                back[dz, chunk] = outs[0] if dz == 0 else shifted(outs[dz], stations, chans, dz, 0)
        out = assemble(
            own, [back[dz, chunk] for dz in range(stations) for chunk in range(CHUNKS)], stations, CHUNKS
        )
    out = out.reshape(reach, stations * here, pairs // LANES, 2, LANES)
    return out.transpose(0, 1, 3, 2, 4).reshape(1, reach, stations * here, 2, pairs)


CHUNKS = 2


def direct(stations, chans):
    return stations == 4 and chans in (1, 2, 4)


def solution(mesh):
    placed = (P(("grp", "stn", "chan"), None, None), P())

    return jax.shard_map(
        local,
        mesh=mesh,
        in_specs=placed,
        out_specs=P(("grp", "stn"), None, "chan", None, None),
        check_vma=False,
    )
```

```python
import functools
import math

import jax
import jax.numpy as jnp
import numpy as np
from jax import lax
from jax.experimental import pallas as pl
from jax.experimental.pallas import tpu as pltpu
from jax.sharding import PartitionSpec as P


AVG = 16
LANES = 128
SUB = 8
f32 = jnp.float32
bf16 = jnp.bfloat16


def add(a, b):
    return b if a is None else a if b is None else a + b


def sub(a, b):
    if b is None:
        return a
    return -b if a is None else a - b


def turn(re, im, num, den):
    num %= den
    if num == 0:
        return re, im
    if 4 * num == den:
        return im, None if re is None else -re
    if 2 * num == den:
        return (None if re is None else -re), (None if im is None else -im)
    if 4 * num == 3 * den:
        return (None if im is None else -im), re
    c = math.cos(2 * math.pi * num / den)
    s = math.sin(2 * math.pi * num / den)
    if 8 * num == den or 8 * num == 5 * den:
        if im is None:
            return re * c, re * -s
        if re is None:
            return im * s, im * c
        return (re + im) * c, (im - re) * c
    if im is None:
        return re * c, re * -s
    if re is None:
        return im * s, im * c
    return re * c + im * s, im * c - re * s


def fft(values, needed):
    size = len(values)
    if size == 1:
        return values
    if all(im is None for _, im in values):
        half_need = size // 4 + 1 if size >= 4 else size // 2
        even = fft(values[0::2], min(half_need, size // 2))
        odd = fft(values[1::2], min(half_need, size // 2))

        def mirrored(part, k):
            n = size // 2
            if k < len(part):
                return part[k]
            re, im = part[n - k]
            return re, (None if im is None else -im)

        out = [None] * size
        for k in range(size // 2):
            if k >= needed and k + size // 2 >= needed:
                continue
            er, ei = mirrored(even, k)
            tr, ti = turn(*mirrored(odd, k), k, size)
            out[k] = (add(er, tr), add(ei, ti))
            out[k + size // 2] = (sub(er, tr), sub(ei, ti))
        return out[:needed]
    even = fft(values[0::2], size // 2)
    odd = fft(values[1::2], size // 2)
    out = [None] * size
    for k in range(size // 2):
        er, ei = even[k]
        tr, ti = turn(*odd[k], k, size)
        out[k] = (add(er, tr), add(ei, ti))
        out[k + size // 2] = (sub(er, tr), sub(ei, ti))
    return out[:needed]


def filtered(x, weights, spectra_count):
    tap_count = len(weights)

    def correlated(h, v, count):
        out = []
        for n in range(count):
            total = h[0] * v[n]
            for k in range(1, len(h)):
                total = total + h[k] * v[n + k]
            out.append(total)
        return out

    if tap_count % 2 or spectra_count % 2:
        return correlated(weights, x, spectra_count)
    even, odd = weights[0::2], weights[1::2]
    first, second = x[0::2], x[1::2]
    count = spectra_count // 2
    need = count + tap_count // 2 - 1
    shared = correlated([e + o for e, o in zip(even, odd)], second, count)
    left = correlated(even, [first[n] - second[n] for n in range(need)], count)
    right = correlated(odd, [first[n + 1] - second[n] for n in range(need)], count)
    out = []
    for n in range(count):
        out += [shared[n] + left[n], shared[n] + right[n]]
    return out


SKEW = SUB + 1


def spectra_kernel(tw_ref, t_ref, x_ref, taps_ref, *refs, sizes, sends, turned):
    inputs, frames, tiles, per_step, spectra_count, tap_count, stations, chans = sizes
    outs = refs[: len(sends)]
    w_ref, a_ref, f_ref, xp_ref, s_ref, z_ref, sems = refs[len(sends) :]
    half = tiles // 2
    kept = LANES // 2
    rows = (half + 1) * spectra_count
    pitch = rows + 4
    block = AVG * spectra_count
    parts = tiles // AVG
    step = pl.program_id(0)

    def one_tile(here, carry):
        lanes = pl.ds(pl.multiple_of(here * LANES, LANES), LANES)
        x = [x_ref[frame, :, lanes].astype(f32) for frame in range(frames)]
        weights = [jnp.broadcast_to(taps_ref[t : t + 1, lanes], (inputs, LANES)) for t in range(tap_count)]
        at = (step * per_step + here) * SUB
        for s, total in enumerate(filtered(x, weights, spectra_count)):
            w_ref[pl.ds(pl.multiple_of(s * tiles * SUB + at, SUB), inputs), :] = total
        return carry

    lax.fori_loop(0, per_step, one_tile, 0)

    @pl.when(step == pl.num_programs(0) - 1)
    def finish():
        radix = 8
        other = tiles // radix
        columns = radix // 2 + 1

        def one_spectrum(s, carry):
            base = s * tiles * SUB
            present = {}
            for b in range(other):
                got = [
                    (w_ref[pl.ds(pl.multiple_of(base + (other * a + b) * SUB, SUB), SUB), :], None)
                    for a in range(radix)
                ]
                for ka, (re, im) in enumerate(fft(got, columns)):
                    if ka:
                        re, im = turn(re, im, ka * b, tiles)
                    for c, value in enumerate((re, im)):
                        present[ka, b, c] = value is not None
                        if value is not None:
                            at = ((ka * other + b) * 2 + c) * SUB
                            a_ref[at : at + SUB, :] = value
            for ka in range(columns):
                got = []
                for b in range(other):
                    at = (ka * other + b) * 2 * SUB
                    got.append(
                        tuple(
                            a_ref[at + c * SUB : at + (c + 1) * SUB, :] if present[ka, b, c] else None
                            for c in range(2)
                        )
                    )
                need = other if 0 < ka else other // 2 + 1
                done = fft(got, need)
                for kb, (re, im) in enumerate(done):
                    direct = ka + radix * kb
                    if direct <= half:
                        k1, conj = direct, False
                    else:
                        k1, conj = tiles - direct, True
                        if k1 % radix == ka:
                            continue
                    if im is None:
                        im = jnp.zeros_like(re)
                    if conj:
                        im = -im
                    cos = tw_ref[k1 * 2 * SUB : (k1 * 2 + 1) * SUB, :]
                    sin = tw_ref[(k1 * 2 + 1) * SUB : (k1 * 2 + 2) * SUB, :]
                    where = k1 * spectra_count + s
                    f_ref[pl.ds(where, SUB, stride=pitch), :] = re * cos + im * sin
                    f_ref[pl.ds(SUB * pitch + where, SUB, stride=pitch), :] = im * cos - re * sin
            return carry

        lax.fori_loop(0, spectra_count, one_spectrum, 0)

        def one_input(one, carry):
            for c in range(2):
                value = f_ref[pl.ds((c * SUB + one) * pitch, rows), :]
                high = value.astype(bf16)
                xp_ref[:, c * LANES : (c + 1) * LANES] = high
                xp_ref[:, (2 + c) * LANES : (3 + c) * LANES] = (value - high.astype(f32)).astype(bf16)
            for j in range(parts):
                if j < parts // 2:
                    first = j * block
                    which = 0
                else:
                    first = ((parts - 1 - j) * AVG + 1) * spectra_count
                    which = 1
                high = xp_ref[first : first + block, : 2 * LANES]
                low = xp_ref[first : first + block, 2 * LANES :]
                dims = (((1,), (1,)), ((), ()))
                both = lax.dot_general(t_ref[which], high, dims, preferred_element_type=f32)
                more = lax.dot_general(t_ref[which, : 2 * kept], low, dims, preferred_element_type=f32)
                out = both[: 2 * kept] + (both[2 * kept :] + more)
                for c in range(2):
                    for h in range(block // LANES):
                        tile = (j * 2 + c) * (block // LANES) + h
                        s_ref[pl.ds(tile * kept * SKEW + one, kept, stride=SKEW), :] = out[
                            c * kept : (c + 1) * kept, h * LANES : (h + 1) * LANES
                        ]
            return carry

        lax.fori_loop(0, inputs, one_input, 0)

        wide = 2 * block // LANES
        near = math.gcd(kept // chans, 2)

        def staged(m):
            for j in range(parts):
                for tile in range(wide):
                    z_ref[m * parts + j, :, tile * LANES : (tile + 1) * LANES] = s_ref[
                        pl.ds(((j * wide + tile) * kept + m) * SKEW, inputs), :
                    ].astype(bf16)

        copies = []
        for dc in range(chans):
            chan = lax.bitwise_xor(lax.axis_index("chan"), dc) if turned else dc

            def some_rows(at, carry, chan=chan):
                for one in range(near):
                    staged(chan * (kept // chans) + at * near + one)
                return carry

            lax.fori_loop(0, kept // chans // near, some_rows, 0)
            for index, (dz, of, skip, count) in enumerate(sends):
                if of != dc:
                    continue
                first = chan * (kept // chans * parts) + skip
                if dz is not None:
                    station = lax.bitwise_xor(lax.axis_index("stn"), dz)
                    first = first + station * (kept // chans * parts // stations)
                copies.append(
                    pltpu.make_async_copy(z_ref.at[pl.ds(first, count)], outs[index], sems.at[index])
                )
                copies[-1].start()
        for copy in copies:
            copy.wait()


def tables(frame_len):
    tiles = frame_len // LANES
    half = tiles // 2
    kept = LANES // 2
    k1 = np.arange(half + 1)[:, None]
    p = np.arange(LANES)[None, :]
    angle = 2 * np.pi * ((k1 * p) % frame_len) / frame_len
    tw = np.stack([np.cos(angle), np.sin(angle)], axis=1)[:, :, None, :]
    tw = np.broadcast_to(tw, (half + 1, 2, SUB, LANES)).reshape(-1, LANES).astype(np.float32)

    def one(m, sign):
        theta = 2 * np.pi * ((m[:, None] * p) % LANES) / LANES
        cos, sin = np.cos(theta), np.sin(theta)
        full = np.concatenate(
            [np.concatenate([cos, sin], axis=1), sign * np.concatenate([-sin, cos], axis=1)], axis=0
        )
        full = (full * frame_len ** (-0.5)).astype(np.float32)
        high = full.astype(jnp.bfloat16)
        low = (full - high.astype(np.float32)).astype(jnp.bfloat16)
        return np.concatenate([high, low], axis=0)

    m = np.arange(kept)
    return tw, np.stack([one(m, 1.0), one(LANES - 1 - m, -1.0)])


HBM = pl.BlockSpec(memory_space=pl.ANY)


def make_spectra(voltages, taps, sends, stations, chans, turned):
    frames, inputs, frame_len = voltages.shape
    tap_count = taps.shape[0]
    spectra_count = frames - tap_count + 1
    tiles = frame_len // LANES
    half = tiles // 2
    rows = (half + 1) * spectra_count
    block = AVG * spectra_count
    groups = frame_len // 2 // AVG
    per_step = 8
    tw, t = tables(frame_len)
    sizes = (inputs, frames, tiles, per_step, spectra_count, tap_count, stations, chans)
    return pl.pallas_call(
        functools.partial(spectra_kernel, sizes=sizes, sends=sends, turned=turned),
        name="spectra",
        grid=(tiles // per_step,),
        in_specs=[
            pl.BlockSpec(tw.shape, lambda q: (0, 0)),
            pl.BlockSpec(t.shape, lambda q: (0, 0, 0)),
            pl.BlockSpec((frames, inputs, per_step * LANES), lambda q: (0, 0, q)),
            pl.BlockSpec((tap_count, per_step * LANES), lambda q: (0, q)),
        ],
        out_specs=[HBM] * len(sends),
        out_shape=[jax.ShapeDtypeStruct((count, inputs, 2 * block), bf16) for _, _, _, count in sends],
        scratch_shapes=[
            pltpu.VMEM((spectra_count * tiles * SUB, LANES), f32),
            pltpu.VMEM((5 * (tiles // 8) * 2 * SUB, LANES), f32),
            pltpu.VMEM((2 * SUB * (rows + 4), LANES), f32),
            pltpu.VMEM((rows, 4 * LANES), bf16),
            pltpu.VMEM((groups * (2 * block // LANES) * SKEW, LANES), f32),
            pltpu.VMEM((groups, inputs, 2 * block), bf16),
            pltpu.SemaphoreType.DMA((len(sends),)),
        ],
    )(jnp.asarray(tw), jnp.asarray(t), voltages, taps)


def lefts(own):
    wide = own.shape[1]
    return [own, jnp.concatenate([own[:, wide // 2 :], -own[:, : wide // 2]], axis=1)]


def products(p_ref, slot, owns):
    right = jnp.concatenate(owns, axis=0)
    left = jnp.concatenate([piece for own in owns for piece in lefts(own)], axis=0)
    out = lax.dot_general(left, right, (((1,), (1,)), ((), ())), preferred_element_type=f32)
    p_ref[slot, :, : right.shape[0]] = out


def tiles_of(p_ref, q_ref, slot, at, block, targets, block_inputs, scale):
    copies = LANES // block_inputs
    out_rows = block_inputs * block_inputs // LANES
    place = lax.broadcasted_iota(jnp.int32, (out_rows, LANES), 1) // block_inputs
    for part in range(2):
        base = (2 * block + part) * block_inputs
        rows = [p_ref[slot, pl.ds(base + r, out_rows, stride=copies), :] for r in range(copies)]
        for index, target in enumerate(targets):
            value = None
            for r in range(copies):
                shift = (r - target) % copies if isinstance(target, int) else lax.rem(r - target + copies, copies)
                moved = rows[r]
                if not (isinstance(shift, int) and shift == 0):
                    moved = pltpu.roll(moved, shift * block_inputs, 1)
                value = moved if r == 0 else jnp.where(place == r, moved, value)
            q_ref[at + index, pl.ds(part, out_rows, stride=2), :] = value * scale
    return [q_ref[at + index].astype(bf16) for index in range(len(targets))]


def correlate_kernel(r_ref, o_ref, p_ref, q_ref, *, sizes):
    stations, chans, reach, scale = sizes

    block_inputs = chans * r_ref.shape[2]

    def one_block(b, carry):
        def fetch(block):
            return jnp.concatenate([r_ref[c * stations + block, 0] for c in range(chans)], axis=0)

        own = fetch(b)
        for d in range(reach):
            other = lax.rem(b + d, stations)
            right = fetch(other)
            left = jnp.concatenate(lefts(own), axis=0)
            p_ref[d, :, :block_inputs] = lax.dot_general(
                left, right, (((1,), (1,)), ((), ())), preferred_element_type=f32
            )
            (tile,) = tiles_of(p_ref, q_ref, d, d, 0, [0], block_inputs, scale)
            o_ref[b, d, 0, :, :] = tile
        return carry

    lax.fori_loop(0, stations, one_block, 0)


def correlate(turned, stations, chans, reach, scale):
    sources, groups, inputs, wide = turned.shape
    block_inputs = chans * inputs
    out_rows = block_inputs * block_inputs // LANES
    return pl.pallas_call(
        functools.partial(correlate_kernel, sizes=(stations, chans, reach, scale)),
        name="correlate",
        grid=(groups,),
        in_specs=[pl.BlockSpec((sources, 1, inputs, wide), lambda g: (0, g, 0, 0))],
        out_specs=pl.BlockSpec((stations, reach, 1, 2 * out_rows, LANES), lambda g: (0, 0, g, 0, 0)),
        out_shape=jax.ShapeDtypeStruct((stations, reach, groups, 2 * out_rows, LANES), bf16),
        scratch_shapes=[
            pltpu.VMEM((reach, 2 * block_inputs, LANES), f32),
            pltpu.VMEM((reach, 2 * out_rows, LANES), f32),
        ],
    )(turned)


def pieces_kernel(*refs, sizes, pieces):
    blocks, chans, groups, distances, scale, per_step = sizes
    arrived = refs[: len(pieces)]
    outs = refs[len(pieces) : len(pieces) + blocks]
    r_ref, p_ref, q_ref = refs[len(pieces) + blocks :]
    here = lax.axis_index("stn") if blocks > 1 else 0
    block_inputs = chans * r_ref.shape[2]
    together = math.gcd(groups, 8)

    def collect(at, carry):
        for index, (dz, dc, mine, first) in enumerate(pieces):
            chan = lax.bitwise_xor(lax.axis_index("chan"), dc)
            block = lax.bitwise_xor(here, dz) if blocks > 1 else 0
            start = first + at * together
            if mine:
                start = start + lax.axis_index("stn") * mine
            r_ref[block * chans + chan, pl.ds(at * together, together), :, :] = arrived[index][
                pl.ds(start, together), :, :
            ]
        return carry

    lax.fori_loop(0, groups // together, collect, 0)

    def some_groups(at, carry):
        for one in range(per_step):
            g = at * per_step + one
            owns = [
                jnp.concatenate([r_ref[block * chans + c, g] for c in range(chans)], axis=0)
                for block in range(blocks)
            ]
            products(p_ref, one, owns)
            for turn_by in range(blocks):
                block = lax.bitwise_xor(here, turn_by) if blocks > 1 else 0
                targets = [lax.rem(block + d, blocks) if blocks > 1 else 0 for d in distances]
                first = (one * blocks + turn_by) * len(distances)
                tiles = tiles_of(p_ref, q_ref, one, first, block, targets, block_inputs, scale)
                for d, tile in enumerate(tiles):
                    outs[turn_by][d, g, :, :] = tile
        return carry

    lax.fori_loop(0, groups // per_step, some_groups, 0)


def correlate_pieces(arrays, pieces, blocks, chans, groups, distances, scale):
    inputs, wide = arrays[0].shape[1:]
    block_inputs = chans * inputs
    out_rows = block_inputs * block_inputs // LANES
    per_step = math.gcd(groups, 8 // blocks)
    sizes = (blocks, chans, groups, distances, scale, per_step)
    shape = (len(distances), groups, 2 * out_rows, LANES)
    vmem = pl.BlockSpec(memory_space=pltpu.VMEM)
    return pl.pallas_call(
        functools.partial(pieces_kernel, sizes=sizes, pieces=pieces),
        in_specs=[vmem] * len(arrays),
        out_specs=[vmem] * blocks,
        out_shape=[jax.ShapeDtypeStruct(shape, bf16)] * blocks,
        scratch_shapes=[
            pltpu.VMEM((blocks * chans, groups, inputs, wide), bf16),
            pltpu.VMEM((per_step, blocks * 2 * block_inputs, LANES), f32),
            pltpu.VMEM((per_step * blocks * len(distances), 2 * out_rows, LANES), f32),
        ],
    )(*arrays)


def assemble_kernel(own_ref, *refs, stations, chunks):
    parts = refs[:-1]
    out_ref = refs[-1]
    out_ref[0, :, :, :] = own_ref[0]
    for dz in range(stations):
        host = lax.bitwise_xor(lax.axis_index("stn"), dz)
        for chunk in range(chunks):
            part = parts[dz * chunks + chunk]
            count = part.shape[1]
            at = (host * chunks + chunk) * count
            for d in range(part.shape[0]):
                out_ref[d + 1, pl.ds(at, count), :, :] = part[d]


def assemble(own, parts, stations, chunks):
    reach = parts[0].shape[0] + 1
    vmem = pl.BlockSpec(memory_space=pltpu.VMEM)
    return pl.pallas_call(
        functools.partial(assemble_kernel, stations=stations, chunks=chunks),
        name="assemble",
        in_specs=[vmem] * (1 + len(parts)),
        out_specs=vmem,
        out_shape=jax.ShapeDtypeStruct((reach,) + own.shape[1:], bf16),
    )(own, *parts)


def shifted(value, stations, chans, dz, dc):
    pairs = [
        (z * chans + c, (z ^ dz) * chans + (c ^ dc))
        for z in range(stations)
        for c in range(chans)
    ]
    return lax.ppermute(value, ("stn", "chan"), pairs)


def local(voltages, taps):
    inputs_here, frames, frame_len = voltages.shape
    spectra_count = frames - taps.shape[0] + 1
    stations = lax.axis_size("stn")
    chans = lax.axis_size("chan")
    reach = stations // 2 + 1
    block_inputs = chans * inputs_here
    pairs = block_inputs * block_inputs
    groups = frame_len // 2 // AVG
    here = groups // (stations * chans)
    scale = 1.0 / (spectra_count * AVG)
    frames_first = voltages.transpose(1, 0, 2)
    if not direct(stations, chans):
        sends = tuple((None, dc, 0, groups // chans) for dc in range(chans))
        slices = make_spectra(frames_first, taps, sends, stations, chans, False)
        send = jnp.concatenate(slices, axis=0).reshape(chans * stations, here, inputs_here, -1)
        turned = lax.all_to_all(send, ("chan", "stn"), 0, 0, tiled=True)
        tiles = correlate(turned, stations, chans, reach, scale)
        back = lax.all_to_all(tiles, "stn", 0, 0, tiled=True)
        out = back.transpose(1, 0, 2, 3, 4)
    else:
        part = here // CHUNKS
        sends = [(None, dc, 0, here * stations) for dc in range(chans)]
        sends += [(dz, dc, 0, here) for dz in (2, 1, 3) for dc in range(chans)]
        sent = make_spectra(frames_first, taps, tuple(sends), stations, chans, True)
        whole, far = [], {}
        for (dz, dc, _, _), value in zip(sends, sent):
            if dz is None:
                whole.append(shifted(value, stations, chans, 0, dc) if dc else value)
            else:
                far[dz, dc] = shifted(value, stations, chans, dz, dc)
        pieces = [(0, dc, 0, 0) for dc in range(chans)]
        (own,) = correlate_pieces(whole, pieces, 1, chans, here * stations, (0,), scale)
        distances = tuple(range(1, reach))
        back = {}
        for chunk in range(CHUNKS):
            pieces = [(0, dc, here, chunk * part) for dc in range(chans)]
            pieces += [(dz, dc, 0, chunk * part) for dz, dc in far]
            arrays = whole + list(far.values())
            outs = correlate_pieces(arrays, pieces, stations, chans, part, distances, scale)
            for dz in range(stations):
                back[dz, chunk] = outs[0] if dz == 0 else shifted(outs[dz], stations, chans, dz, 0)
        out = assemble(
            own, [back[dz, chunk] for dz in range(stations) for chunk in range(CHUNKS)], stations, CHUNKS
        )
    out = out.reshape(reach, stations * here, pairs // LANES, 2, LANES)
    return out.transpose(0, 1, 3, 2, 4).reshape(1, reach, stations * here, 2, pairs)


CHUNKS = 2


def direct(stations, chans):
    return stations == 4 and chans in (1, 2, 4)


def solution(mesh):
    placed = (P(("grp", "stn", "chan"), None, None), P())

    return jax.shard_map(
        local,
        mesh=mesh,
        in_specs=placed,
        out_specs=P(("grp", "stn"), None, "chan", None, None),
        check_vma=False,
    )
```

```python
import functools
import math

import jax
import jax.numpy as jnp
import numpy as np
from jax import lax
from jax.experimental import pallas as pl
from jax.experimental.pallas import tpu as pltpu
from jax.sharding import PartitionSpec as P


AVG = 16
LANES = 128
SUB = 8
f32 = jnp.float32
bf16 = jnp.bfloat16


def add(a, b):
    return b if a is None else a if b is None else a + b


def sub(a, b):
    if b is None:
        return a
    return -b if a is None else a - b


def turn(re, im, num, den):
    num %= den
    if num == 0:
        return re, im
    if 4 * num == den:
        return im, None if re is None else -re
    if 2 * num == den:
        return (None if re is None else -re), (None if im is None else -im)
    if 4 * num == 3 * den:
        return (None if im is None else -im), re
    c = math.cos(2 * math.pi * num / den)
    s = math.sin(2 * math.pi * num / den)
    if 8 * num == den or 8 * num == 5 * den:
        if im is None:
            return re * c, re * -s
        if re is None:
            return im * s, im * c
        return (re + im) * c, (im - re) * c
    if im is None:
        return re * c, re * -s
    if re is None:
        return im * s, im * c
    return re * c + im * s, im * c - re * s


def fft(values, needed):
    size = len(values)
    if size == 1:
        return values
    if all(im is None for _, im in values):
        half_need = size // 4 + 1 if size >= 4 else size // 2
        even = fft(values[0::2], min(half_need, size // 2))
        odd = fft(values[1::2], min(half_need, size // 2))

        def mirrored(part, k):
            n = size // 2
            if k < len(part):
                return part[k]
            re, im = part[n - k]
            return re, (None if im is None else -im)

        out = [None] * size
        for k in range(size // 2):
            if k >= needed and k + size // 2 >= needed:
                continue
            er, ei = mirrored(even, k)
            tr, ti = turn(*mirrored(odd, k), k, size)
            out[k] = (add(er, tr), add(ei, ti))
            out[k + size // 2] = (sub(er, tr), sub(ei, ti))
        return out[:needed]
    even = fft(values[0::2], size // 2)
    odd = fft(values[1::2], size // 2)
    out = [None] * size
    for k in range(size // 2):
        er, ei = even[k]
        tr, ti = turn(*odd[k], k, size)
        out[k] = (add(er, tr), add(ei, ti))
        out[k + size // 2] = (sub(er, tr), sub(ei, ti))
    return out[:needed]


def filtered(x, weights, spectra_count):
    tap_count = len(weights)

    def correlated(h, v, count):
        out = []
        for n in range(count):
            total = h[0] * v[n]
            for k in range(1, len(h)):
                total = total + h[k] * v[n + k]
            out.append(total)
        return out

    if tap_count % 2 or spectra_count % 2:
        return correlated(weights, x, spectra_count)
    even, odd = weights[0::2], weights[1::2]
    first, second = x[0::2], x[1::2]
    count = spectra_count // 2
    need = count + tap_count // 2 - 1
    shared = correlated([e + o for e, o in zip(even, odd)], second, count)
    left = correlated(even, [first[n] - second[n] for n in range(need)], count)
    right = correlated(odd, [first[n + 1] - second[n] for n in range(need)], count)
    out = []
    for n in range(count):
        out += [shared[n] + left[n], shared[n] + right[n]]
    return out


SKEW = SUB + 1


def spectra_kernel(tw_ref, t_ref, x_ref, taps_ref, *refs, sizes, sends, merged, turned):
    inputs, first_frame, tiles, per_step, spectra_count, tap_count, stations, chans = sizes
    earlier = refs[: len(merged)]
    outs = refs[len(merged) : len(merged) + len(sends)]
    w_ref, a_ref, f_ref, xp_ref, s_ref, z_ref, sems = refs[len(merged) + len(sends) :]
    half = tiles // 2
    kept = LANES // 2
    rows = (half + 1) * spectra_count
    pitch = rows + 4
    block = AVG * spectra_count
    parts = tiles // AVG
    step = pl.program_id(0)

    def one_tile(here, carry):
        lanes = pl.ds(pl.multiple_of(here * LANES, LANES), LANES)
        frames = range(first_frame, first_frame + spectra_count + tap_count - 1)
        x = [x_ref[frame, :, lanes].astype(f32) for frame in frames]
        weights = [jnp.broadcast_to(taps_ref[t : t + 1, lanes], (inputs, LANES)) for t in range(tap_count)]
        at = (step * per_step + here) * SUB
        for s, total in enumerate(filtered(x, weights, spectra_count)):
            w_ref[pl.ds(pl.multiple_of(s * tiles * SUB + at, SUB), inputs), :] = total
        return carry

    lax.fori_loop(0, per_step, one_tile, 0)

    @pl.when(step == pl.num_programs(0) - 1)
    def finish():
        radix = 8
        other = tiles // radix
        columns = radix // 2 + 1

        def one_spectrum(s, carry):
            base = s * tiles * SUB
            present = {}
            for b in range(other):
                got = [
                    (w_ref[pl.ds(pl.multiple_of(base + (other * a + b) * SUB, SUB), SUB), :], None)
                    for a in range(radix)
                ]
                for ka, (re, im) in enumerate(fft(got, columns)):
                    if ka:
                        re, im = turn(re, im, ka * b, tiles)
                    for c, value in enumerate((re, im)):
                        present[ka, b, c] = value is not None
                        if value is not None:
                            at = ((ka * other + b) * 2 + c) * SUB
                            a_ref[at : at + SUB, :] = value
            for ka in range(columns):
                got = []
                for b in range(other):
                    at = (ka * other + b) * 2 * SUB
                    got.append(
                        tuple(
                            a_ref[at + c * SUB : at + (c + 1) * SUB, :] if present[ka, b, c] else None
                            for c in range(2)
                        )
                    )
                need = other if 0 < ka else other // 2 + 1
                done = fft(got, need)
                for kb, (re, im) in enumerate(done):
                    direct = ka + radix * kb
                    if direct <= half:
                        k1, conj = direct, False
                    else:
                        k1, conj = tiles - direct, True
                        if k1 % radix == ka:
                            continue
                    if im is None:
                        im = jnp.zeros_like(re)
                    if conj:
                        im = -im
                    cos = tw_ref[k1 * 2 * SUB : (k1 * 2 + 1) * SUB, :]
                    sin = tw_ref[(k1 * 2 + 1) * SUB : (k1 * 2 + 2) * SUB, :]
                    where = k1 * spectra_count + s
                    f_ref[pl.ds(where, SUB, stride=pitch), :] = re * cos + im * sin
                    f_ref[pl.ds(SUB * pitch + where, SUB, stride=pitch), :] = im * cos - re * sin
            return carry

        lax.fori_loop(0, spectra_count, one_spectrum, 0)

        def one_input(one, carry):
            for c in range(2):
                value = f_ref[pl.ds((c * SUB + one) * pitch, rows), :]
                high = value.astype(bf16)
                xp_ref[:, c * LANES : (c + 1) * LANES] = high
                xp_ref[:, (2 + c) * LANES : (3 + c) * LANES] = (value - high.astype(f32)).astype(bf16)
            dims = (((1,), (1,)), ((), ()))
            for which in range(2):
                first = which * spectra_count
                high = xp_ref[first : first + parts // 2 * block, : 2 * LANES]
                low = xp_ref[first : first + parts // 2 * block, 2 * LANES :]
                both = lax.dot_general(t_ref[which], high, dims, preferred_element_type=f32)
                more = lax.dot_general(t_ref[which, : 2 * kept], low, dims, preferred_element_type=f32)
                out = both[: 2 * kept] + (both[2 * kept :] + more)
                for u in range(parts // 2):
                    j = parts - 1 - u if which else u
                    for c in range(2):
                        for h in range(block // LANES):
                            tile = (j * 2 + c) * (block // LANES) + h
                            at = u * block + h * LANES
                            s_ref[pl.ds(tile * kept * SKEW + one, kept, stride=SKEW), :] = out[
                                c * kept : (c + 1) * kept, at : at + LANES
                            ]
            return carry

        lax.fori_loop(0, inputs, one_input, 0)

        wide = 2 * block // LANES
        near = math.gcd(kept // chans, 2)

        def staged(m):
            for j in range(parts):
                for tile in range(wide):
                    z_ref[m * parts + j, :, tile * LANES : (tile + 1) * LANES] = s_ref[
                        pl.ds(((j * wide + tile) * kept + m) * SKEW, inputs), :
                    ].astype(bf16)

        copies = []
        for index, which in enumerate(merged):
            copies.append(
                pltpu.make_async_copy(
                    earlier[index],
                    outs[which].at[:, :, pl.ds(0, wide * LANES)],
                    sems.at[len(sends) + index],
                )
            )
            copies[-1].start()
        for dc in range(chans):
            chan = lax.bitwise_xor(lax.axis_index("chan"), dc) if turned else dc

            def some_rows(at, carry, chan=chan):
                for one in range(near):
                    staged(chan * (kept // chans) + at * near + one)
                return carry

            lax.fori_loop(0, kept // chans // near, some_rows, 0)
            for index, (dz, of, count) in enumerate(sends):
                if of != dc:
                    continue
                first = chan * (kept // chans * parts)
                if dz is not None:
                    station = lax.bitwise_xor(lax.axis_index("stn"), dz)
                    first = first + station * (kept // chans * parts // stations)
                to = outs[index]
                if index in merged:
                    to = to.at[:, :, pl.ds(wide * LANES, wide * LANES)]
                copies.append(pltpu.make_async_copy(z_ref.at[pl.ds(first, count)], to, sems.at[index]))
                copies[-1].start()
        for copy in copies:
            copy.wait()


def tables(frame_len):
    tiles = frame_len // LANES
    half = tiles // 2
    kept = LANES // 2
    k1 = np.arange(half + 1)[:, None]
    p = np.arange(LANES)[None, :]
    angle = 2 * np.pi * ((k1 * p) % frame_len) / frame_len
    tw = np.stack([np.cos(angle), np.sin(angle)], axis=1)[:, :, None, :]
    tw = np.broadcast_to(tw, (half + 1, 2, SUB, LANES)).reshape(-1, LANES).astype(np.float32)

    def one(m, sign):
        theta = 2 * np.pi * ((m[:, None] * p) % LANES) / LANES
        cos, sin = np.cos(theta), np.sin(theta)
        full = np.concatenate(
            [np.concatenate([cos, sin], axis=1), sign * np.concatenate([-sin, cos], axis=1)], axis=0
        )
        full = (full * frame_len ** (-0.5)).astype(np.float32)
        high = full.astype(jnp.bfloat16)
        low = (full - high.astype(np.float32)).astype(jnp.bfloat16)
        return np.concatenate([high, low], axis=0)

    m = np.arange(kept)
    return tw, np.stack([one(m, 1.0), one(LANES - 1 - m, -1.0)])


HBM = pl.BlockSpec(memory_space=pl.ANY)


def make_spectra(voltages, taps, sends, stations, chans, turned, first_frame=0, halves=1, merged=()):
    frames, inputs, frame_len = voltages.shape
    tap_count = taps.shape[0]
    spectra_count = (frames - tap_count + 1) // halves
    tiles = frame_len // LANES
    half = tiles // 2
    rows = (half + 1) * spectra_count
    block = AVG * spectra_count
    groups = frame_len // 2 // AVG
    per_step = 8
    tw, t = tables(frame_len)
    sizes = (inputs, first_frame, tiles, per_step, spectra_count, tap_count, stations, chans)
    places = tuple(index for index, _ in merged)
    shapes = [
        jax.ShapeDtypeStruct((count, inputs, (4 if index in places else 2) * block), bf16)
        for index, (_, _, count) in enumerate(sends)
    ]
    return pl.pallas_call(
        functools.partial(spectra_kernel, sizes=sizes, sends=sends, merged=places, turned=turned),
        name="spectra",
        grid=(tiles // per_step,),
        in_specs=[
            pl.BlockSpec(tw.shape, lambda q: (0, 0)),
            pl.BlockSpec(t.shape, lambda q: (0, 0, 0)),
            pl.BlockSpec((frames, inputs, per_step * LANES), lambda q: (0, 0, q)),
            pl.BlockSpec((tap_count, per_step * LANES), lambda q: (0, q)),
        ]
        + [pl.BlockSpec(value.shape, lambda q: (0, 0, 0)) for _, value in merged],
        out_specs=[HBM] * len(sends),
        out_shape=shapes,
        scratch_shapes=[
            pltpu.VMEM((spectra_count * tiles * SUB, LANES), f32),
            pltpu.VMEM((5 * (tiles // 8) * 2 * SUB, LANES), f32),
            pltpu.VMEM((2 * SUB * (rows + 4), LANES), f32),
            pltpu.VMEM((rows, 4 * LANES), bf16),
            pltpu.VMEM((groups * (2 * block // LANES) * SKEW, LANES), f32),
            pltpu.VMEM((groups, inputs, 2 * block), bf16),
            pltpu.SemaphoreType.DMA((len(sends) + len(merged),)),
        ],
    )(jnp.asarray(tw), jnp.asarray(t), voltages, taps, *[value for _, value in merged])


def lefts(own, halves):
    width = own.shape[1] // (2 * halves)
    crossed = []
    for half in range(halves):
        at = 2 * half * width
        crossed += [own[:, at + width : at + 2 * width], -own[:, at : at + width]]
    return [own, jnp.concatenate(crossed, axis=1)]


def products(p_ref, slot, owns, halves):
    right = jnp.concatenate(owns, axis=0)
    left = jnp.concatenate([piece for own in owns for piece in lefts(own, halves)], axis=0)
    out = lax.dot_general(left, right, (((1,), (1,)), ((), ())), preferred_element_type=f32)
    p_ref[slot, :, : right.shape[0]] = out


def tiles_of(p_ref, q_ref, slot, at, block, targets, block_inputs, scale):
    copies = LANES // block_inputs
    out_rows = block_inputs * block_inputs // LANES
    place = lax.broadcasted_iota(jnp.int32, (out_rows, LANES), 1) // block_inputs
    for part in range(2):
        base = (2 * block + part) * block_inputs
        rows = [p_ref[slot, pl.ds(base + r, out_rows, stride=copies), :] for r in range(copies)]
        for index, target in enumerate(targets):
            value = None
            for r in range(copies):
                shift = (r - target) % copies if isinstance(target, int) else lax.rem(r - target + copies, copies)
                moved = rows[r]
                if not (isinstance(shift, int) and shift == 0):
                    moved = pltpu.roll(moved, shift * block_inputs, 1)
                value = moved if r == 0 else jnp.where(place == r, moved, value)
            q_ref[at + index, pl.ds(part, out_rows, stride=2), :] = value * scale
    return [q_ref[at + index].astype(bf16) for index in range(len(targets))]


def correlate_kernel(r_ref, o_ref, p_ref, q_ref, *, sizes):
    stations, chans, reach, scale = sizes

    block_inputs = chans * r_ref.shape[2]

    def one_block(b, carry):
        def fetch(block):
            return jnp.concatenate([r_ref[c * stations + block, 0] for c in range(chans)], axis=0)

        own = fetch(b)
        for d in range(reach):
            other = lax.rem(b + d, stations)
            right = fetch(other)
            left = jnp.concatenate(lefts(own, 1), axis=0)
            p_ref[d, :, :block_inputs] = lax.dot_general(
                left, right, (((1,), (1,)), ((), ())), preferred_element_type=f32
            )
            (tile,) = tiles_of(p_ref, q_ref, d, d, 0, [0], block_inputs, scale)
            o_ref[b, d, 0, :, :] = tile
        return carry

    lax.fori_loop(0, stations, one_block, 0)


def correlate(turned, stations, chans, reach, scale):
    sources, groups, inputs, wide = turned.shape
    block_inputs = chans * inputs
    out_rows = block_inputs * block_inputs // LANES
    return pl.pallas_call(
        functools.partial(correlate_kernel, sizes=(stations, chans, reach, scale)),
        name="correlate",
        grid=(groups,),
        in_specs=[pl.BlockSpec((sources, 1, inputs, wide), lambda g: (0, g, 0, 0))],
        out_specs=pl.BlockSpec((stations, reach, 1, 2 * out_rows, LANES), lambda g: (0, 0, g, 0, 0)),
        out_shape=jax.ShapeDtypeStruct((stations, reach, groups, 2 * out_rows, LANES), bf16),
        scratch_shapes=[
            pltpu.VMEM((reach, 2 * block_inputs, LANES), f32),
            pltpu.VMEM((reach, 2 * out_rows, LANES), f32),
        ],
    )(turned)


def pieces_kernel(*refs, sizes, pieces):
    blocks, chans, groups, distances, scale, per_step = sizes
    arrived = refs[: len(pieces)]
    outs = refs[len(pieces) : len(pieces) + blocks]
    r_ref, p_ref, q_ref, sems = refs[len(pieces) + blocks :]
    here = lax.axis_index("stn") if blocks > 1 else 0
    block_inputs = chans * r_ref.shape[2]
    stages = 2
    part = groups // stages
    copies = []
    for stage in range(stages):
        for index, (dz, dc, mine, lane) in enumerate(pieces):
            chan = lax.bitwise_xor(lax.axis_index("chan"), dc)
            block = lax.bitwise_xor(here, dz) if blocks > 1 else 0
            start = stage * part
            if mine:
                start = start + lax.axis_index("stn") * mine
            copies.append(
                pltpu.make_async_copy(
                    arrived[index].at[pl.ds(start, part)],
                    r_ref.at[
                        block * chans + chan,
                        pl.ds(stage * part, part),
                        :,
                        pl.ds(lane, arrived[index].shape[-1]),
                    ],
                    sems.at[stage * len(pieces) + index],
                )
            )
            copies[-1].start()

    def some_groups(at, carry):
        for one in range(per_step):
            g = at * per_step + one
            owns = [
                jnp.concatenate([r_ref[block * chans + c, g] for c in range(chans)], axis=0)
                for block in range(blocks)
            ]
            products(p_ref, one, owns, HALVES)
            for turn_by in range(blocks):
                block = lax.bitwise_xor(here, turn_by) if blocks > 1 else 0
                targets = [lax.rem(block + d, blocks) if blocks > 1 else 0 for d in distances]
                first = (one * blocks + turn_by) * len(distances)
                tiles = tiles_of(p_ref, q_ref, one, first, block, targets, block_inputs, scale)
                for d, tile in enumerate(tiles):
                    outs[turn_by][d, g, :, :] = tile
        return carry

    for stage in range(stages):
        for copy in copies[stage * len(pieces) : (stage + 1) * len(pieces)]:
            copy.wait()
        lax.fori_loop(stage * part // per_step, (stage + 1) * part // per_step, some_groups, 0)


def correlate_pieces(arrays, pieces, blocks, chans, groups, distances, scale):
    inputs = arrays[0].shape[1]
    wide = max(lane + value.shape[2] for value, (_, _, _, lane) in zip(arrays, pieces))
    block_inputs = chans * inputs
    out_rows = block_inputs * block_inputs // LANES
    per_step = math.gcd(groups // 2, 8 // blocks)
    sizes = (blocks, chans, groups, distances, scale, per_step)
    shape = (len(distances), groups, 2 * out_rows, LANES)
    return pl.pallas_call(
        functools.partial(pieces_kernel, sizes=sizes, pieces=pieces),
        in_specs=[HBM] * len(arrays),
        out_specs=[pl.BlockSpec(memory_space=pltpu.VMEM)] * blocks,
        out_shape=[jax.ShapeDtypeStruct(shape, bf16)] * blocks,
        scratch_shapes=[
            pltpu.VMEM((blocks * chans, groups, inputs, wide), bf16),
            pltpu.VMEM((per_step, blocks * 2 * block_inputs, LANES), f32),
            pltpu.VMEM((per_step * blocks * len(distances), 2 * out_rows, LANES), f32),
            pltpu.SemaphoreType.DMA((2 * len(pieces),)),
        ],
    )(*arrays)


def assemble_kernel(own_ref, *refs, stations, chunks):
    parts = refs[:-1]
    out_ref = refs[-1]
    out_ref[0, :, :, :] = own_ref[0]
    for dz in range(stations):
        host = lax.bitwise_xor(lax.axis_index("stn"), dz)
        for chunk in range(chunks):
            part = parts[dz * chunks + chunk]
            count = part.shape[1]
            at = (host * chunks + chunk) * count
            for d in range(part.shape[0]):
                out_ref[d + 1, pl.ds(at, count), :, :] = part[d]


def assemble(own, parts, stations, chunks):
    reach = parts[0].shape[0] + 1
    vmem = pl.BlockSpec(memory_space=pltpu.VMEM)
    return pl.pallas_call(
        functools.partial(assemble_kernel, stations=stations, chunks=chunks),
        name="assemble",
        in_specs=[vmem] * (1 + len(parts)),
        out_specs=vmem,
        out_shape=jax.ShapeDtypeStruct((reach,) + own.shape[1:], bf16),
    )(own, *parts)


def shifted(value, stations, chans, dz, dc):
    pairs = [
        (z * chans + c, (z ^ dz) * chans + (c ^ dc))
        for z in range(stations)
        for c in range(chans)
    ]
    return lax.ppermute(value, ("stn", "chan"), pairs)


def local(voltages, taps):
    inputs_here, frames, frame_len = voltages.shape
    spectra_count = frames - taps.shape[0] + 1
    stations = lax.axis_size("stn")
    chans = lax.axis_size("chan")
    reach = stations // 2 + 1
    block_inputs = chans * inputs_here
    pairs = block_inputs * block_inputs
    groups = frame_len // 2 // AVG
    here = groups // (stations * chans)
    scale = 1.0 / (spectra_count * AVG)
    frames_first = voltages.transpose(1, 0, 2)
    if not direct(stations, chans):
        sends = tuple((None, dc, groups // chans) for dc in range(chans))
        slices = make_spectra(frames_first, taps, sends, stations, chans, False)
        send = jnp.concatenate(slices, axis=0).reshape(chans * stations, here, inputs_here, -1)
        turned = lax.all_to_all(send, ("chan", "stn"), 0, 0, tiled=True)
        tiles = correlate(turned, stations, chans, reach, scale)
        back = lax.all_to_all(tiles, "stn", 0, 0, tiled=True)
        out = back.transpose(1, 0, 2, 3, 4)
    else:
        near = [(None, dc, here * stations) for dc in range(chans)]
        far = [(dz, dc, here) for dz in (2, 3) for dc in range(chans)]
        mid = [(1, dc, here) for dc in range(chans)]
        sends = tuple(far + near + mid)
        own_pieces, own_arrays, pieces, arrays = [], [], [], []
        kept_back = ()
        for half in range(HALVES):
            sent = make_spectra(
                frames_first,
                taps,
                sends,
                stations,
                chans,
                True,
                half * spectra_count // HALVES,
                HALVES,
                kept_back,
            )
            if half == 0:
                kept_back = tuple((len(far + near) + index, value) for index, value in enumerate(sent[-chans:]))
            lane = half * 2 * AVG * spectra_count // HALVES
            for (dz, dc, _), value in zip(sends, sent):
                if dz == 1 and half == 0:
                    continue
                moved = value if dz is None and dc == 0 else shifted(value, stations, chans, dz or 0, dc)
                if dz is None:
                    own_pieces.append((0, dc, 0, lane))
                    own_arrays.append(moved)
                pieces.append((dz or 0, dc, here if dz is None else 0, 0 if dz == 1 else lane))
                arrays.append(moved)
        (own,) = correlate_pieces(own_arrays, own_pieces, 1, chans, here * stations, (0,), scale)
        outs = correlate_pieces(arrays, pieces, stations, chans, here, tuple(range(1, reach)), scale)
        back = [outs[dz] if dz == 0 else shifted(outs[dz], stations, chans, dz, 0) for dz in range(stations)]
        out = assemble(own, back, stations, 1)
    out = out.reshape(reach, stations * here, pairs // LANES, 2, LANES)
    return out.transpose(0, 1, 3, 2, 4).reshape(1, reach, stations * here, 2, pairs)


HALVES = 2


def direct(stations, chans):
    return stations == 4 and chans in (1, 2, 4)


def solution(mesh):
    placed = (P(("grp", "stn", "chan"), None, None), P())

    return jax.shard_map(
        local,
        mesh=mesh,
        in_specs=placed,
        out_specs=P(("grp", "stn"), None, "chan", None, None),
        check_vma=False,
    )
```

```python
import functools
import math

import jax
import jax.numpy as jnp
import numpy as np
from jax import lax
from jax.experimental import pallas as pl
from jax.experimental.pallas import tpu as pltpu
from jax.sharding import PartitionSpec as P


AVG = 16
LANES = 128
SUB = 8
f32 = jnp.float32
bf16 = jnp.bfloat16


def add(a, b):
    return b if a is None else a if b is None else a + b


def sub(a, b):
    if b is None:
        return a
    return -b if a is None else a - b


def turn(re, im, num, den):
    num %= den
    if num == 0:
        return re, im
    if 4 * num == den:
        return im, None if re is None else -re
    if 2 * num == den:
        return (None if re is None else -re), (None if im is None else -im)
    if 4 * num == 3 * den:
        return (None if im is None else -im), re
    c = math.cos(2 * math.pi * num / den)
    s = math.sin(2 * math.pi * num / den)
    if 8 * num == den or 8 * num == 5 * den:
        if im is None:
            return re * c, re * -s
        if re is None:
            return im * s, im * c
        return (re + im) * c, (im - re) * c
    if im is None:
        return re * c, re * -s
    if re is None:
        return im * s, im * c
    return re * c + im * s, im * c - re * s


def fft(values, needed):
    size = len(values)
    if size == 1:
        return values
    if all(im is None for _, im in values):
        half_need = size // 4 + 1 if size >= 4 else size // 2
        even = fft(values[0::2], min(half_need, size // 2))
        odd = fft(values[1::2], min(half_need, size // 2))

        def mirrored(part, k):
            n = size // 2
            if k < len(part):
                return part[k]
            re, im = part[n - k]
            return re, (None if im is None else -im)

        out = [None] * size
        for k in range(size // 2):
            if k >= needed and k + size // 2 >= needed:
                continue
            er, ei = mirrored(even, k)
            tr, ti = turn(*mirrored(odd, k), k, size)
            out[k] = (add(er, tr), add(ei, ti))
            out[k + size // 2] = (sub(er, tr), sub(ei, ti))
        return out[:needed]
    even = fft(values[0::2], size // 2)
    odd = fft(values[1::2], size // 2)
    out = [None] * size
    for k in range(size // 2):
        er, ei = even[k]
        tr, ti = turn(*odd[k], k, size)
        out[k] = (add(er, tr), add(ei, ti))
        out[k + size // 2] = (sub(er, tr), sub(ei, ti))
    return out[:needed]


def filtered(x, weights, spectra_count):
    tap_count = len(weights)

    def correlated(h, v, count):
        out = []
        for n in range(count):
            total = h[0] * v[n]
            for k in range(1, len(h)):
                total = total + h[k] * v[n + k]
            out.append(total)
        return out

    if tap_count % 2 or spectra_count % 2:
        return correlated(weights, x, spectra_count)
    even, odd = weights[0::2], weights[1::2]
    first, second = x[0::2], x[1::2]
    count = spectra_count // 2
    need = count + tap_count // 2 - 1
    shared = correlated([e + o for e, o in zip(even, odd)], second, count)
    left = correlated(even, [first[n] - second[n] for n in range(need)], count)
    right = correlated(odd, [first[n + 1] - second[n] for n in range(need)], count)
    out = []
    for n in range(count):
        out += [shared[n] + left[n], shared[n] + right[n]]
    return out


SKEW = SUB + 1


def spectra_kernel(tw_ref, t_ref, x_ref, taps_ref, *refs, sizes, sends, merged, turned):
    inputs, first_frame, tiles, per_step, spectra_count, tap_count, stations, chans = sizes
    earlier = refs[: len(merged)]
    outs = refs[len(merged) : len(merged) + len(sends)]
    w_ref, a_ref, f_ref, xp_ref, s_ref, z_ref, sems = refs[len(merged) + len(sends) :]
    half = tiles // 2
    kept = LANES // 2
    rows = (half + 1) * spectra_count
    pitch = rows + 4
    block = AVG * spectra_count
    parts = tiles // AVG
    step = pl.program_id(0)

    def one_tile(here, carry):
        lanes = pl.ds(pl.multiple_of(here * LANES, LANES), LANES)
        frames = range(first_frame, first_frame + spectra_count + tap_count - 1)
        x = [x_ref[frame, :, lanes].astype(f32) for frame in frames]
        weights = [jnp.broadcast_to(taps_ref[t : t + 1, lanes], (inputs, LANES)) for t in range(tap_count)]
        at = (step * per_step + here) * SUB
        for s, total in enumerate(filtered(x, weights, spectra_count)):
            w_ref[pl.ds(pl.multiple_of(s * tiles * SUB + at, SUB), inputs), :] = total
        return carry

    lax.fori_loop(0, per_step, one_tile, 0)

    @pl.when(step == pl.num_programs(0) - 1)
    def finish():
        radix = 8
        other = tiles // radix
        columns = radix // 2 + 1

        def one_spectrum(s, carry):
            base = s * tiles * SUB
            present = {}
            for b in range(other):
                got = [
                    (w_ref[pl.ds(pl.multiple_of(base + (other * a + b) * SUB, SUB), SUB), :], None)
                    for a in range(radix)
                ]
                for ka, (re, im) in enumerate(fft(got, columns)):
                    if ka:
                        re, im = turn(re, im, ka * b, tiles)
                    for c, value in enumerate((re, im)):
                        present[ka, b, c] = value is not None
                        if value is not None:
                            at = ((ka * other + b) * 2 + c) * SUB
                            a_ref[at : at + SUB, :] = value
            for ka in range(columns):
                got = []
                for b in range(other):
                    at = (ka * other + b) * 2 * SUB
                    got.append(
                        tuple(
                            a_ref[at + c * SUB : at + (c + 1) * SUB, :] if present[ka, b, c] else None
                            for c in range(2)
                        )
                    )
                need = other if 0 < ka else other // 2 + 1
                done = fft(got, need)
                for kb, (re, im) in enumerate(done):
                    direct = ka + radix * kb
                    if direct <= half:
                        k1, conj = direct, False
                    else:
                        k1, conj = tiles - direct, True
                        if k1 % radix == ka:
                            continue
                    if im is None:
                        im = jnp.zeros_like(re)
                    if conj:
                        im = -im
                    cos = tw_ref[k1 * 2 * SUB : (k1 * 2 + 1) * SUB, :]
                    sin = tw_ref[(k1 * 2 + 1) * SUB : (k1 * 2 + 2) * SUB, :]
                    where = k1 * spectra_count + s
                    f_ref[pl.ds(where, SUB, stride=pitch), :] = re * cos + im * sin
                    f_ref[pl.ds(SUB * pitch + where, SUB, stride=pitch), :] = im * cos - re * sin
            return carry

        lax.fori_loop(0, spectra_count, one_spectrum, 0)

        def one_input(one, carry):
            for c in range(2):
                value = f_ref[pl.ds((c * SUB + one) * pitch, rows), :]
                high = value.astype(bf16)
                xp_ref[:, c * LANES : (c + 1) * LANES] = high
                xp_ref[:, (2 + c) * LANES : (3 + c) * LANES] = (value - high.astype(f32)).astype(bf16)
            dims = (((1,), (1,)), ((), ()))
            for which in range(2):
                first = which * spectra_count
                high = xp_ref[first : first + parts // 2 * block, : 2 * LANES]
                low = xp_ref[first : first + parts // 2 * block, 2 * LANES :]
                both = lax.dot_general(t_ref[which], high, dims, preferred_element_type=f32)
                more = lax.dot_general(t_ref[which, : 2 * kept], low, dims, preferred_element_type=f32)
                out = both[: 2 * kept] + (both[2 * kept :] + more)
                for u in range(parts // 2):
                    j = parts - 1 - u if which else u
                    for c in range(2):
                        for h in range(block // LANES):
                            tile = (j * 2 + c) * (block // LANES) + h
                            at = u * block + h * LANES
                            s_ref[pl.ds(tile * kept * SKEW + one, kept, stride=SKEW), :] = out[
                                c * kept : (c + 1) * kept, at : at + LANES
                            ]
            return carry

        lax.fori_loop(0, inputs, one_input, 0)

        wide = 2 * block // LANES
        near = math.gcd(kept // chans, 2)

        def staged(m):
            for j in range(parts):
                for tile in range(wide):
                    z_ref[m * parts + j, :, tile * LANES : (tile + 1) * LANES] = s_ref[
                        pl.ds(((j * wide + tile) * kept + m) * SKEW, inputs), :
                    ].astype(bf16)

        copies = []
        for index, which in enumerate(merged):
            copies.append(
                pltpu.make_async_copy(
                    earlier[index],
                    outs[which].at[:, :, pl.ds(0, wide * LANES)],
                    sems.at[len(sends) + index],
                )
            )
            copies[-1].start()
        for dc in range(chans):
            chan = lax.bitwise_xor(lax.axis_index("chan"), dc) if turned else dc

            def some_rows(at, carry, chan=chan):
                for one in range(near):
                    staged(chan * (kept // chans) + at * near + one)
                return carry

            lax.fori_loop(0, kept // chans // near, some_rows, 0)
            for index, (dz, of, skip, count) in enumerate(sends):
                if of != dc:
                    continue
                first = chan * (kept // chans * parts) + skip
                if dz is not None:
                    station = lax.bitwise_xor(lax.axis_index("stn"), dz)
                    first = first + station * (kept // chans * parts // stations)
                to = outs[index]
                if index in merged:
                    to = to.at[:, :, pl.ds(wide * LANES, wide * LANES)]
                copies.append(pltpu.make_async_copy(z_ref.at[pl.ds(first, count)], to, sems.at[index]))
                copies[-1].start()
        for copy in copies:
            copy.wait()


def tables(frame_len):
    tiles = frame_len // LANES
    half = tiles // 2
    kept = LANES // 2
    k1 = np.arange(half + 1)[:, None]
    p = np.arange(LANES)[None, :]
    angle = 2 * np.pi * ((k1 * p) % frame_len) / frame_len
    tw = np.stack([np.cos(angle), np.sin(angle)], axis=1)[:, :, None, :]
    tw = np.broadcast_to(tw, (half + 1, 2, SUB, LANES)).reshape(-1, LANES).astype(np.float32)

    def one(m, sign):
        theta = 2 * np.pi * ((m[:, None] * p) % LANES) / LANES
        cos, sin = np.cos(theta), np.sin(theta)
        full = np.concatenate(
            [np.concatenate([cos, sin], axis=1), sign * np.concatenate([-sin, cos], axis=1)], axis=0
        )
        full = (full * frame_len ** (-0.5)).astype(np.float32)
        high = full.astype(jnp.bfloat16)
        low = (full - high.astype(np.float32)).astype(jnp.bfloat16)
        return np.concatenate([high, low], axis=0)

    m = np.arange(kept)
    return tw, np.stack([one(m, 1.0), one(LANES - 1 - m, -1.0)])


HBM = pl.BlockSpec(memory_space=pl.ANY)


def make_spectra(voltages, taps, sends, stations, chans, turned, first_frame=0, halves=1, merged=()):
    frames, inputs, frame_len = voltages.shape
    tap_count = taps.shape[0]
    spectra_count = (frames - tap_count + 1) // halves
    tiles = frame_len // LANES
    half = tiles // 2
    rows = (half + 1) * spectra_count
    block = AVG * spectra_count
    groups = frame_len // 2 // AVG
    per_step = 8
    tw, t = tables(frame_len)
    sizes = (inputs, first_frame, tiles, per_step, spectra_count, tap_count, stations, chans)
    places = tuple(index for index, _ in merged)
    shapes = [
        jax.ShapeDtypeStruct((count, inputs, (4 if index in places else 2) * block), bf16)
        for index, (_, _, _, count) in enumerate(sends)
    ]
    return pl.pallas_call(
        functools.partial(spectra_kernel, sizes=sizes, sends=sends, merged=places, turned=turned),
        name="spectra",
        grid=(tiles // per_step,),
        in_specs=[
            pl.BlockSpec(tw.shape, lambda q: (0, 0)),
            pl.BlockSpec(t.shape, lambda q: (0, 0, 0)),
            pl.BlockSpec((frames, inputs, per_step * LANES), lambda q: (0, 0, q)),
            pl.BlockSpec((tap_count, per_step * LANES), lambda q: (0, q)),
        ]
        + [pl.BlockSpec(value.shape, lambda q: (0, 0, 0)) for _, value in merged],
        out_specs=[HBM] * len(sends),
        out_shape=shapes,
        scratch_shapes=[
            pltpu.VMEM((spectra_count * tiles * SUB, LANES), f32),
            pltpu.VMEM((5 * (tiles // 8) * 2 * SUB, LANES), f32),
            pltpu.VMEM((2 * SUB * (rows + 4), LANES), f32),
            pltpu.VMEM((rows, 4 * LANES), bf16),
            pltpu.VMEM((groups * (2 * block // LANES) * SKEW, LANES), f32),
            pltpu.VMEM((groups, inputs, 2 * block), bf16),
            pltpu.SemaphoreType.DMA((len(sends) + len(merged),)),
        ],
    )(jnp.asarray(tw), jnp.asarray(t), voltages, taps, *[value for _, value in merged])


def lefts(own, halves):
    width = own.shape[1] // (2 * halves)
    crossed = []
    for half in range(halves):
        at = 2 * half * width
        crossed += [own[:, at + width : at + 2 * width], -own[:, at : at + width]]
    return [own, jnp.concatenate(crossed, axis=1)]


def products(p_ref, slot, owns, halves):
    right = jnp.concatenate(owns, axis=0)
    left = jnp.concatenate([piece for own in owns for piece in lefts(own, halves)], axis=0)
    out = lax.dot_general(left, right, (((1,), (1,)), ((), ())), preferred_element_type=f32)
    p_ref[slot, :, : right.shape[0]] = out


def tiles_of(p_ref, q_ref, slot, at, block, targets, block_inputs, scale):
    copies = LANES // block_inputs
    out_rows = block_inputs * block_inputs // LANES
    place = lax.broadcasted_iota(jnp.int32, (out_rows, LANES), 1) // block_inputs
    for part in range(2):
        base = (2 * block + part) * block_inputs
        rows = [p_ref[slot, pl.ds(base + r, out_rows, stride=copies), :] for r in range(copies)]
        for index, target in enumerate(targets):
            value = None
            for r in range(copies):
                shift = (r - target) % copies if isinstance(target, int) else lax.rem(r - target + copies, copies)
                moved = rows[r]
                if not (isinstance(shift, int) and shift == 0):
                    moved = pltpu.roll(moved, shift * block_inputs, 1)
                value = moved if r == 0 else jnp.where(place == r, moved, value)
            q_ref[at + index, pl.ds(part, out_rows, stride=2), :] = value * scale
    return [q_ref[at + index].astype(bf16) for index in range(len(targets))]


def correlate_kernel(r_ref, o_ref, p_ref, q_ref, *, sizes):
    stations, chans, reach, scale = sizes

    block_inputs = chans * r_ref.shape[2]

    def one_block(b, carry):
        def fetch(block):
            return jnp.concatenate([r_ref[c * stations + block, 0] for c in range(chans)], axis=0)

        own = fetch(b)
        for d in range(reach):
            other = lax.rem(b + d, stations)
            right = fetch(other)
            left = jnp.concatenate(lefts(own, 1), axis=0)
            p_ref[d, :, :block_inputs] = lax.dot_general(
                left, right, (((1,), (1,)), ((), ())), preferred_element_type=f32
            )
            (tile,) = tiles_of(p_ref, q_ref, d, d, 0, [0], block_inputs, scale)
            o_ref[b, d, 0, :, :] = tile
        return carry

    lax.fori_loop(0, stations, one_block, 0)


def correlate(turned, stations, chans, reach, scale):
    sources, groups, inputs, wide = turned.shape
    block_inputs = chans * inputs
    out_rows = block_inputs * block_inputs // LANES
    return pl.pallas_call(
        functools.partial(correlate_kernel, sizes=(stations, chans, reach, scale)),
        name="correlate",
        grid=(groups,),
        in_specs=[pl.BlockSpec((sources, 1, inputs, wide), lambda g: (0, g, 0, 0))],
        out_specs=pl.BlockSpec((stations, reach, 1, 2 * out_rows, LANES), lambda g: (0, 0, g, 0, 0)),
        out_shape=jax.ShapeDtypeStruct((stations, reach, groups, 2 * out_rows, LANES), bf16),
        scratch_shapes=[
            pltpu.VMEM((reach, 2 * block_inputs, LANES), f32),
            pltpu.VMEM((reach, 2 * out_rows, LANES), f32),
        ],
    )(turned)


def pieces_kernel(*refs, sizes, pieces):
    blocks, chans, groups, distances, scale, per_step = sizes
    arrived = refs[: len(pieces)]
    outs = refs[len(pieces) : len(pieces) + blocks]
    r_ref, p_ref, q_ref, sems = refs[len(pieces) + blocks :]
    here = lax.axis_index("stn") if blocks > 1 else 0
    block_inputs = chans * r_ref.shape[2]
    stages = 2
    part = groups // stages
    copies = []
    for stage in range(stages):
        for index, (dz, dc, mine, first) in enumerate(pieces):
            chan = lax.bitwise_xor(lax.axis_index("chan"), dc)
            block = lax.bitwise_xor(here, dz) if blocks > 1 else 0
            start = first + stage * part
            if mine:
                start = start + lax.axis_index("stn") * mine
            copies.append(
                pltpu.make_async_copy(
                    arrived[index].at[pl.ds(start, part)],
                    r_ref.at[block * chans + chan, pl.ds(stage * part, part)],
                    sems.at[stage * len(pieces) + index],
                )
            )
            copies[-1].start()

    def some_groups(at, carry):
        for one in range(per_step):
            g = at * per_step + one
            owns = [
                jnp.concatenate([r_ref[block * chans + c, g] for c in range(chans)], axis=0)
                for block in range(blocks)
            ]
            products(p_ref, one, owns, HALVES)
            for turn_by in range(blocks):
                block = lax.bitwise_xor(here, turn_by) if blocks > 1 else 0
                targets = [lax.rem(block + d, blocks) if blocks > 1 else 0 for d in distances]
                first = (one * blocks + turn_by) * len(distances)
                tiles = tiles_of(p_ref, q_ref, one, first, block, targets, block_inputs, scale)
                for d, tile in enumerate(tiles):
                    outs[turn_by][d, g, :, :] = tile
        return carry

    for stage in range(stages):
        for copy in copies[stage * len(pieces) : (stage + 1) * len(pieces)]:
            copy.wait()
        lax.fori_loop(stage * part // per_step, (stage + 1) * part // per_step, some_groups, 0)


def correlate_pieces(arrays, pieces, blocks, chans, groups, distances, scale):
    inputs, wide = arrays[0].shape[1:]
    block_inputs = chans * inputs
    out_rows = block_inputs * block_inputs // LANES
    per_step = math.gcd(groups // 2, 8 // blocks)
    sizes = (blocks, chans, groups, distances, scale, per_step)
    shape = (len(distances), groups, 2 * out_rows, LANES)
    return pl.pallas_call(
        functools.partial(pieces_kernel, sizes=sizes, pieces=pieces),
        in_specs=[HBM] * len(arrays),
        out_specs=[pl.BlockSpec(memory_space=pltpu.VMEM)] * blocks,
        out_shape=[jax.ShapeDtypeStruct(shape, bf16)] * blocks,
        scratch_shapes=[
            pltpu.VMEM((blocks * chans, groups, inputs, wide), bf16),
            pltpu.VMEM((per_step, blocks * 2 * block_inputs, LANES), f32),
            pltpu.VMEM((per_step * blocks * len(distances), 2 * out_rows, LANES), f32),
            pltpu.SemaphoreType.DMA((2 * len(pieces),)),
        ],
    )(*arrays)


def assemble_kernel(own_ref, *refs, stations, chunks):
    parts = refs[:-1]
    out_ref = refs[-1]
    out_ref[0, :, :, :] = own_ref[0]
    for dz in range(stations):
        host = lax.bitwise_xor(lax.axis_index("stn"), dz)
        for chunk in range(chunks):
            part = parts[dz * chunks + chunk]
            count = part.shape[1]
            at = (host * chunks + chunk) * count
            for d in range(part.shape[0]):
                out_ref[d + 1, pl.ds(at, count), :, :] = part[d]


def assemble(own, parts, stations, chunks):
    reach = parts[0].shape[0] + 1
    vmem = pl.BlockSpec(memory_space=pltpu.VMEM)
    return pl.pallas_call(
        functools.partial(assemble_kernel, stations=stations, chunks=chunks),
        name="assemble",
        in_specs=[vmem] * (1 + len(parts)),
        out_specs=vmem,
        out_shape=jax.ShapeDtypeStruct((reach,) + own.shape[1:], bf16),
    )(own, *parts)


def shifted(value, stations, chans, dz, dc):
    pairs = [
        (z * chans + c, (z ^ dz) * chans + (c ^ dc))
        for z in range(stations)
        for c in range(chans)
    ]
    return lax.ppermute(value, ("stn", "chan"), pairs)


def local(voltages, taps):
    inputs_here, frames, frame_len = voltages.shape
    spectra_count = frames - taps.shape[0] + 1
    stations = lax.axis_size("stn")
    chans = lax.axis_size("chan")
    reach = stations // 2 + 1
    block_inputs = chans * inputs_here
    pairs = block_inputs * block_inputs
    groups = frame_len // 2 // AVG
    here = groups // (stations * chans)
    scale = 1.0 / (spectra_count * AVG)
    frames_first = voltages.transpose(1, 0, 2)
    if not direct(stations, chans):
        sends = tuple((None, dc, 0, groups // chans) for dc in range(chans))
        slices = make_spectra(frames_first, taps, sends, stations, chans, False)
        send = jnp.concatenate(slices, axis=0).reshape(chans * stations, here, inputs_here, -1)
        turned = lax.all_to_all(send, ("chan", "stn"), 0, 0, tiled=True)
        tiles = correlate(turned, stations, chans, reach, scale)
        back = lax.all_to_all(tiles, "stn", 0, 0, tiled=True)
        out = back.transpose(1, 0, 2, 3, 4)
    else:
        part = here // CHUNKS
        sends = [(dz, dc, chunk * part, part) for chunk in range(CHUNKS) for dz in (2, 3) for dc in range(chans)]
        sends += [(None, dc, 0, here * stations) for dc in range(chans)]
        sends += [(1, dc, 0, here) for dc in range(chans)]
        sent = make_spectra(frames_first, taps, tuple(sends), stations, chans, True)
        got = {}
        for (dz, dc, skip, _), value in zip(sends, sent):
            stays = dz is None and dc == 0
            got[dz, dc, skip // part] = value if stays else shifted(value, stations, chans, dz or 0, dc)
        pieces = [(0, dc, 0, 0) for dc in range(chans)]
        arrays = [got[None, dc, 0] for dc in range(chans)]
        (own,) = correlate_pieces(arrays, pieces, 1, chans, here * stations, (0,), scale)
        back = {}
        for chunk in range(CHUNKS):
            pieces, arrays = [], []
            for (dz, dc, which), value in got.items():
                if dz in (2, 3) and which != chunk:
                    continue
                pieces.append((dz or 0, dc, 0 if dz else here, 0 if dz in (2, 3) else chunk * part))
                arrays.append(value)
            outs = correlate_pieces(arrays, pieces, stations, chans, part, tuple(range(1, reach)), scale)
            for dz in range(stations):
                back[dz, chunk] = outs[dz] if dz == 0 else shifted(outs[dz], stations, chans, dz, 0)
        parts = [back[dz, chunk] for dz in range(stations) for chunk in range(CHUNKS)]
        out = assemble(own, parts, stations, CHUNKS)
    out = out.reshape(reach, stations * here, pairs // LANES, 2, LANES)
    return out.transpose(0, 1, 3, 2, 4).reshape(1, reach, stations * here, 2, pairs)


HALVES = 1
CHUNKS = 2


def direct(stations, chans):
    return stations == 4 and chans in (1, 2, 4)


def solution(mesh):
    placed = (P(("grp", "stn", "chan"), None, None), P())

    return jax.shard_map(
        local,
        mesh=mesh,
        in_specs=placed,
        out_specs=P(("grp", "stn"), None, "chan", None, None),
        check_vma=False,
    )
```

```python
import functools
import math

import jax
import jax.numpy as jnp
import numpy as np
from jax import lax
from jax.experimental import pallas as pl
from jax.experimental.pallas import tpu as pltpu
from jax.sharding import PartitionSpec as P


AVG = 16
LANES = 128
SUB = 8
f32 = jnp.float32
bf16 = jnp.bfloat16


def add(a, b):
    return b if a is None else a if b is None else a + b


def sub(a, b):
    if b is None:
        return a
    return -b if a is None else a - b


def turn(re, im, num, den):
    num %= den
    if num == 0:
        return re, im
    if 4 * num == den:
        return im, None if re is None else -re
    if 2 * num == den:
        return (None if re is None else -re), (None if im is None else -im)
    if 4 * num == 3 * den:
        return (None if im is None else -im), re
    c = math.cos(2 * math.pi * num / den)
    s = math.sin(2 * math.pi * num / den)
    if 8 * num == den or 8 * num == 5 * den:
        if im is None:
            return re * c, re * -s
        if re is None:
            return im * s, im * c
        return (re + im) * c, (im - re) * c
    if im is None:
        return re * c, re * -s
    if re is None:
        return im * s, im * c
    return re * c + im * s, im * c - re * s


def fft(values, needed):
    size = len(values)
    if size == 1:
        return values
    if all(im is None for _, im in values):
        half_need = size // 4 + 1 if size >= 4 else size // 2
        even = fft(values[0::2], min(half_need, size // 2))
        odd = fft(values[1::2], min(half_need, size // 2))

        def mirrored(part, k):
            n = size // 2
            if k < len(part):
                return part[k]
            re, im = part[n - k]
            return re, (None if im is None else -im)

        out = [None] * size
        for k in range(size // 2):
            if k >= needed and k + size // 2 >= needed:
                continue
            er, ei = mirrored(even, k)
            tr, ti = turn(*mirrored(odd, k), k, size)
            out[k] = (add(er, tr), add(ei, ti))
            out[k + size // 2] = (sub(er, tr), sub(ei, ti))
        return out[:needed]
    even = fft(values[0::2], size // 2)
    odd = fft(values[1::2], size // 2)
    out = [None] * size
    for k in range(size // 2):
        er, ei = even[k]
        tr, ti = turn(*odd[k], k, size)
        out[k] = (add(er, tr), add(ei, ti))
        out[k + size // 2] = (sub(er, tr), sub(ei, ti))
    return out[:needed]


def filtered(x, weights, spectra_count):
    tap_count = len(weights)

    def correlated(h, v, count):
        out = []
        for n in range(count):
            total = h[0] * v[n]
            for k in range(1, len(h)):
                total = total + h[k] * v[n + k]
            out.append(total)
        return out

    if tap_count % 2 or spectra_count % 2:
        return correlated(weights, x, spectra_count)
    even, odd = weights[0::2], weights[1::2]
    first, second = x[0::2], x[1::2]
    count = spectra_count // 2
    need = count + tap_count // 2 - 1
    shared = correlated([e + o for e, o in zip(even, odd)], second, count)
    left = correlated(even, [first[n] - second[n] for n in range(need)], count)
    right = correlated(odd, [first[n + 1] - second[n] for n in range(need)], count)
    out = []
    for n in range(count):
        out += [shared[n] + left[n], shared[n] + right[n]]
    return out


SKEW = SUB + 1


def spectra_kernel(tw_ref, t_ref, x_ref, taps_ref, *refs, sizes, sends, turned):
    inputs, first_frame, tiles, per_step, spectra_count, tap_count, stations, chans = sizes
    outs = refs[: len(sends)]
    w_ref, a_ref, f_ref, xp_ref, s_ref, z_ref, sems = refs[len(sends) :]
    half = tiles // 2
    kept = LANES // 2
    rows = (half + 1) * spectra_count
    pitch = rows + 4
    block = AVG * spectra_count
    parts = tiles // AVG
    step = pl.program_id(0)

    def one_tile(here, carry):
        lanes = pl.ds(pl.multiple_of(here * LANES, LANES), LANES)
        frames = range(first_frame, first_frame + spectra_count + tap_count - 1)
        x = [x_ref[frame, :, lanes].astype(f32) for frame in frames]
        weights = [jnp.broadcast_to(taps_ref[t : t + 1, lanes], (inputs, LANES)) for t in range(tap_count)]
        at = (step * per_step + here) * SUB
        for s, total in enumerate(filtered(x, weights, spectra_count)):
            w_ref[pl.ds(pl.multiple_of(s * tiles * SUB + at, SUB), inputs), :] = total
        return carry

    lax.fori_loop(0, per_step, one_tile, 0)

    @pl.when(step == pl.num_programs(0) - 1)
    def finish():
        radix = 8
        other = tiles // radix
        columns = radix // 2 + 1

        def one_spectrum(s, carry):
            base = s * tiles * SUB
            present = {}
            for b in range(other):
                got = [
                    (w_ref[pl.ds(pl.multiple_of(base + (other * a + b) * SUB, SUB), SUB), :], None)
                    for a in range(radix)
                ]
                for ka, (re, im) in enumerate(fft(got, columns)):
                    if ka:
                        re, im = turn(re, im, ka * b, tiles)
                    for c, value in enumerate((re, im)):
                        present[ka, b, c] = value is not None
                        if value is not None:
                            at = ((ka * other + b) * 2 + c) * SUB
                            a_ref[at : at + SUB, :] = value
            for ka in range(columns):
                got = []
                for b in range(other):
                    at = (ka * other + b) * 2 * SUB
                    got.append(
                        tuple(
                            a_ref[at + c * SUB : at + (c + 1) * SUB, :] if present[ka, b, c] else None
                            for c in range(2)
                        )
                    )
                need = other if 0 < ka else other // 2 + 1
                done = fft(got, need)
                for kb, (re, im) in enumerate(done):
                    direct = ka + radix * kb
                    if direct <= half:
                        k1, conj = direct, False
                    else:
                        k1, conj = tiles - direct, True
                        if k1 % radix == ka:
                            continue
                    if im is None:
                        im = jnp.zeros_like(re)
                    if conj:
                        im = -im
                    cos = tw_ref[k1 * 2 * SUB : (k1 * 2 + 1) * SUB, :]
                    sin = tw_ref[(k1 * 2 + 1) * SUB : (k1 * 2 + 2) * SUB, :]
                    where = k1 * spectra_count + s
                    f_ref[pl.ds(where, SUB, stride=pitch), :] = re * cos + im * sin
                    f_ref[pl.ds(SUB * pitch + where, SUB, stride=pitch), :] = im * cos - re * sin
            return carry

        lax.fori_loop(0, spectra_count, one_spectrum, 0)

        def one_input(one, carry):
            for c in range(2):
                value = f_ref[pl.ds((c * SUB + one) * pitch, rows), :]
                high = value.astype(bf16)
                xp_ref[:, c * LANES : (c + 1) * LANES] = high
                xp_ref[:, (2 + c) * LANES : (3 + c) * LANES] = (value - high.astype(f32)).astype(bf16)
            dims = (((1,), (1,)), ((), ()))
            for which in range(2):
                first = which * spectra_count
                high = xp_ref[first : first + parts // 2 * block, : 2 * LANES]
                low = xp_ref[first : first + parts // 2 * block, 2 * LANES :]
                both = lax.dot_general(t_ref[which], high, dims, preferred_element_type=f32)
                more = lax.dot_general(t_ref[which, : 2 * kept], low, dims, preferred_element_type=f32)
                out = both[: 2 * kept] + (both[2 * kept :] + more)
                for u in range(parts // 2):
                    j = parts - 1 - u if which else u
                    for c in range(2):
                        for h in range(block // LANES):
                            tile = (j * 2 + c) * (block // LANES) + h
                            at = u * block + h * LANES
                            s_ref[pl.ds(tile * kept * SKEW + one, kept, stride=SKEW), :] = out[
                                c * kept : (c + 1) * kept, at : at + LANES
                            ]
            return carry

        lax.fori_loop(0, inputs, one_input, 0)

        wide = 2 * block // LANES
        near = math.gcd(kept // chans, 2)

        def staged(m):
            for j in range(parts):
                for tile in range(wide):
                    z_ref[m * parts + j, :, tile * LANES : (tile + 1) * LANES] = s_ref[
                        pl.ds(((j * wide + tile) * kept + m) * SKEW, inputs), :
                    ].astype(bf16)

        copies = []
        for dc in range(chans):
            chan = lax.bitwise_xor(lax.axis_index("chan"), dc) if turned else dc

            def some_rows(at, carry, chan=chan):
                for one in range(near):
                    staged(chan * (kept // chans) + at * near + one)
                return carry

            lax.fori_loop(0, kept // chans // near, some_rows, 0)
            for index, (dzs, of, skip, count) in enumerate(sends):
                if of != dc:
                    continue
                for at, dz in enumerate(dzs):
                    first = chan * (kept // chans * parts) + skip
                    if dz is not None:
                        station = lax.bitwise_xor(lax.axis_index("stn"), dz)
                        first = first + station * (kept // chans * parts // stations)
                    copies.append(
                        pltpu.make_async_copy(
                            z_ref.at[pl.ds(first, count)],
                            outs[index].at[pl.ds(at * count, count)],
                            sems.at[len(copies)],
                        )
                    )
                    copies[-1].start()
        for copy in copies:
            copy.wait()


def tables(frame_len):
    tiles = frame_len // LANES
    half = tiles // 2
    kept = LANES // 2
    k1 = np.arange(half + 1)[:, None]
    p = np.arange(LANES)[None, :]
    angle = 2 * np.pi * ((k1 * p) % frame_len) / frame_len
    tw = np.stack([np.cos(angle), np.sin(angle)], axis=1)[:, :, None, :]
    tw = np.broadcast_to(tw, (half + 1, 2, SUB, LANES)).reshape(-1, LANES).astype(np.float32)

    def one(m, sign):
        theta = 2 * np.pi * ((m[:, None] * p) % LANES) / LANES
        cos, sin = np.cos(theta), np.sin(theta)
        full = np.concatenate(
            [np.concatenate([cos, sin], axis=1), sign * np.concatenate([-sin, cos], axis=1)], axis=0
        )
        full = (full * frame_len ** (-0.5)).astype(np.float32)
        high = full.astype(jnp.bfloat16)
        low = (full - high.astype(np.float32)).astype(jnp.bfloat16)
        return np.concatenate([high, low], axis=0)

    m = np.arange(kept)
    return tw, np.stack([one(m, 1.0), one(LANES - 1 - m, -1.0)])


HBM = pl.BlockSpec(memory_space=pl.ANY)


def make_spectra(voltages, taps, sends, stations, chans, turned):
    frames, inputs, frame_len = voltages.shape
    tap_count = taps.shape[0]
    spectra_count = frames - tap_count + 1
    tiles = frame_len // LANES
    half = tiles // 2
    rows = (half + 1) * spectra_count
    block = AVG * spectra_count
    groups = frame_len // 2 // AVG
    per_step = 8
    tw, t = tables(frame_len)
    sizes = (inputs, 0, tiles, per_step, spectra_count, tap_count, stations, chans)
    shapes = [jax.ShapeDtypeStruct((len(dzs) * count, inputs, 2 * block), bf16) for dzs, _, _, count in sends]
    return pl.pallas_call(
        functools.partial(spectra_kernel, sizes=sizes, sends=sends, turned=turned),
        name="spectra",
        grid=(tiles // per_step,),
        in_specs=[
            pl.BlockSpec(tw.shape, lambda q: (0, 0)),
            pl.BlockSpec(t.shape, lambda q: (0, 0, 0)),
            pl.BlockSpec((frames, inputs, per_step * LANES), lambda q: (0, 0, q)),
            pl.BlockSpec((tap_count, per_step * LANES), lambda q: (0, q)),
        ],
        out_specs=[HBM] * len(sends),
        out_shape=shapes,
        scratch_shapes=[
            pltpu.VMEM((spectra_count * tiles * SUB, LANES), f32),
            pltpu.VMEM((5 * (tiles // 8) * 2 * SUB, LANES), f32),
            pltpu.VMEM((2 * SUB * (rows + 4), LANES), f32),
            pltpu.VMEM((rows, 4 * LANES), bf16),
            pltpu.VMEM((groups * (2 * block // LANES) * SKEW, LANES), f32),
            pltpu.VMEM((groups, inputs, 2 * block), bf16),
            pltpu.SemaphoreType.DMA((sum(len(dzs) for dzs, _, _, _ in sends),)),
        ],
    )(jnp.asarray(tw), jnp.asarray(t), voltages, taps)


def lefts(own, halves):
    width = own.shape[1] // (2 * halves)
    crossed = []
    for half in range(halves):
        at = 2 * half * width
        crossed += [own[:, at + width : at + 2 * width], -own[:, at : at + width]]
    return [own, jnp.concatenate(crossed, axis=1)]


def products(p_ref, slot, owns, halves):
    right = jnp.concatenate(owns, axis=0)
    left = jnp.concatenate([piece for own in owns for piece in lefts(own, halves)], axis=0)
    out = lax.dot_general(left, right, (((1,), (1,)), ((), ())), preferred_element_type=f32)
    p_ref[slot, :, : right.shape[0]] = out


def tiles_of(p_ref, q_ref, slot, at, block, targets, block_inputs, scale):
    copies = LANES // block_inputs
    out_rows = block_inputs * block_inputs // LANES
    place = lax.broadcasted_iota(jnp.int32, (out_rows, LANES), 1) // block_inputs
    for part in range(2):
        base = (2 * block + part) * block_inputs
        rows = [p_ref[slot, pl.ds(base + r, out_rows, stride=copies), :] for r in range(copies)]
        for index, target in enumerate(targets):
            value = None
            for r in range(copies):
                shift = (r - target) % copies if isinstance(target, int) else lax.rem(r - target + copies, copies)
                moved = rows[r]
                if not (isinstance(shift, int) and shift == 0):
                    moved = pltpu.roll(moved, shift * block_inputs, 1)
                value = moved if r == 0 else jnp.where(place == r, moved, value)
            q_ref[at + index, pl.ds(part, out_rows, stride=2), :] = value * scale
    return [q_ref[at + index].astype(bf16) for index in range(len(targets))]


def correlate_kernel(r_ref, o_ref, p_ref, q_ref, *, sizes):
    stations, chans, reach, scale = sizes

    block_inputs = chans * r_ref.shape[2]

    def one_block(b, carry):
        def fetch(block):
            return jnp.concatenate([r_ref[c * stations + block, 0] for c in range(chans)], axis=0)

        own = fetch(b)
        for d in range(reach):
            other = lax.rem(b + d, stations)
            right = fetch(other)
            left = jnp.concatenate(lefts(own, 1), axis=0)
            p_ref[d, :, :block_inputs] = lax.dot_general(
                left, right, (((1,), (1,)), ((), ())), preferred_element_type=f32
            )
            (tile,) = tiles_of(p_ref, q_ref, d, d, 0, [0], block_inputs, scale)
            o_ref[b, d, 0, :, :] = tile
        return carry

    lax.fori_loop(0, stations, one_block, 0)


def correlate(turned, stations, chans, reach, scale):
    sources, groups, inputs, wide = turned.shape
    block_inputs = chans * inputs
    out_rows = block_inputs * block_inputs // LANES
    return pl.pallas_call(
        functools.partial(correlate_kernel, sizes=(stations, chans, reach, scale)),
        name="correlate",
        grid=(groups,),
        in_specs=[pl.BlockSpec((sources, 1, inputs, wide), lambda g: (0, g, 0, 0))],
        out_specs=pl.BlockSpec((stations, reach, 1, 2 * out_rows, LANES), lambda g: (0, 0, g, 0, 0)),
        out_shape=jax.ShapeDtypeStruct((stations, reach, groups, 2 * out_rows, LANES), bf16),
        scratch_shapes=[
            pltpu.VMEM((reach, 2 * block_inputs, LANES), f32),
            pltpu.VMEM((reach, 2 * out_rows, LANES), f32),
        ],
    )(turned)


def pieces_kernel(*refs, sizes, pieces, stages):
    count, blocks, chans, distances, scale, per_step = sizes
    arrived = refs[:count]
    outs = refs[count : count + blocks]
    r_ref, p_ref, q_ref, sems = refs[count + blocks :]
    here = lax.axis_index("stn") if blocks > 1 else 0
    block_inputs = chans * r_ref.shape[2]
    copies = []
    for first, last in stages:
        for index, dz, dc, mine, source, at, groups in pieces:
            if not first <= at < last:
                continue
            block = lax.bitwise_xor(here, dz) if blocks > 1 else 0
            if mine:
                source = source + lax.axis_index("stn") * mine
            if dc is None:
                moved = arrived[index].at[:, pl.ds(source, groups)]
                to = r_ref.at[pl.ds(block * chans, chans), pl.ds(at, groups)]
            else:
                chan = lax.bitwise_xor(lax.axis_index("chan"), dc)
                moved = arrived[index].at[pl.ds(source, groups)]
                to = r_ref.at[block * chans + chan, pl.ds(at, groups)]
            copies.append(pltpu.make_async_copy(moved, to, sems.at[len(copies)]))
            copies[-1].start()

    def some_groups(at, carry):
        for one in range(per_step):
            g = at * per_step + one
            owns = [
                jnp.concatenate([r_ref[block * chans + c, g] for c in range(chans)], axis=0)
                for block in range(blocks)
            ]
            products(p_ref, one, owns, HALVES)
            for turn_by in range(blocks):
                block = lax.bitwise_xor(here, turn_by) if blocks > 1 else 0
                targets = [lax.rem(block + d, blocks) if blocks > 1 else 0 for d in distances]
                first = (one * blocks + turn_by) * len(distances)
                tiles = tiles_of(p_ref, q_ref, one, first, block, targets, block_inputs, scale)
                for d, tile in enumerate(tiles):
                    outs[turn_by][d, g, :, :] = tile
        return carry

    done = 0
    for first, last in stages:
        many = sum(first <= piece[5] < last for piece in pieces)
        for copy in copies[done : done + many]:
            copy.wait()
        done += many
        lax.fori_loop(first // per_step, last // per_step, some_groups, 0)


def correlate_pieces(arrays, pieces, stages, blocks, chans, distances, scale):
    inputs, wide = arrays[0].shape[-2:]
    block_inputs = chans * inputs
    out_rows = block_inputs * block_inputs // LANES
    groups = stages[-1][1]
    per_step = math.gcd(*(edge for stage in stages for edge in stage), 8 // blocks)
    sizes = (len(arrays), blocks, chans, distances, scale, per_step)
    shape = (len(distances), groups, 2 * out_rows, LANES)
    return pl.pallas_call(
        functools.partial(pieces_kernel, sizes=sizes, pieces=tuple(pieces), stages=stages),
        in_specs=[HBM] * len(arrays),
        out_specs=[pl.BlockSpec(memory_space=pltpu.VMEM)] * blocks,
        out_shape=[jax.ShapeDtypeStruct(shape, bf16)] * blocks,
        scratch_shapes=[
            pltpu.VMEM((blocks * chans, groups, inputs, wide), bf16),
            pltpu.VMEM((per_step, blocks * 2 * block_inputs, LANES), f32),
            pltpu.VMEM((per_step * blocks * len(distances), 2 * out_rows, LANES), f32),
            pltpu.SemaphoreType.DMA((len(pieces),)),
        ],
    )(*arrays)


def pack_kernel(*refs, cuts, chans, here):
    slices = refs[:chans]
    outs = refs[chans : chans + len(cuts)]
    sems = refs[chans + len(cuts)]
    copies = []
    for out, (dz, skip, count) in zip(outs, cuts):
        first = lax.bitwise_xor(lax.axis_index("stn"), dz) * here + skip
        for dc in range(chans):
            chan = lax.bitwise_xor(lax.axis_index("chan"), dc)
            copies.append(
                pltpu.make_async_copy(slices[dc].at[pl.ds(first, count)], out.at[chan], sems.at[len(copies)])
            )
            copies[-1].start()
    for copy in copies:
        copy.wait()


def pack(slices, cuts, here):
    chans = len(slices)
    return pl.pallas_call(
        functools.partial(pack_kernel, cuts=cuts, chans=chans, here=here),
        name="pack",
        in_specs=[HBM] * chans,
        out_specs=[pl.BlockSpec(memory_space=pltpu.VMEM)] * len(cuts),
        out_shape=[jax.ShapeDtypeStruct((chans, count) + slices[0].shape[1:], bf16) for _, _, count in cuts],
        scratch_shapes=[pltpu.SemaphoreType.DMA((len(cuts) * chans,))],
    )(*slices)


def assemble_kernel(own_ref, *refs, places, here):
    parts = refs[:-1]
    out_ref = refs[-1]
    out_ref[0] = own_ref[0]
    for part, (dz, skip) in zip(parts, places):
        host = lax.bitwise_xor(lax.axis_index("stn"), dz)
        for d in range(part.shape[0]):
            out_ref[d + 1, pl.ds(host * here + skip, part.shape[1]), :, :] = part[d]


def assemble(own, parts, places, here):
    reach = parts[0].shape[0] + 1
    vmem = pl.BlockSpec(memory_space=pltpu.VMEM)
    return pl.pallas_call(
        functools.partial(assemble_kernel, places=places, here=here),
        name="assemble",
        in_specs=[vmem] * (1 + len(parts)),
        out_specs=vmem,
        out_shape=jax.ShapeDtypeStruct((reach,) + own.shape[1:], bf16),
    )(own, *parts)


def shifted(value, stations, chans, dz, dc):
    pairs = [
        (z * chans + c, (z ^ dz) * chans + (c ^ dc))
        for z in range(stations)
        for c in range(chans)
    ]
    return lax.ppermute(value, ("stn", "chan"), pairs)


def local(voltages, taps):
    inputs_here, frames, frame_len = voltages.shape
    spectra_count = frames - taps.shape[0] + 1
    stations = lax.axis_size("stn")
    chans = lax.axis_size("chan")
    reach = stations // 2 + 1
    block_inputs = chans * inputs_here
    pairs = block_inputs * block_inputs
    groups = frame_len // 2 // AVG
    here = groups // (stations * chans)
    scale = 1.0 / (spectra_count * AVG)
    frames_first = voltages.transpose(1, 0, 2)
    if not direct(stations, chans):
        sends = tuple(((None,), dc, 0, groups // chans) for dc in range(chans))
        slices = make_spectra(frames_first, taps, sends, stations, chans, False)
        send = jnp.concatenate(slices, axis=0).reshape(chans * stations, here, inputs_here, -1)
        turned = lax.all_to_all(send, ("chan", "stn"), 0, 0, tiled=True)
        tiles = correlate(turned, stations, chans, reach, scale)
        back = lax.all_to_all(tiles, "stn", 0, 0, tiled=True)
        out = back.transpose(1, 0, 2, 3, 4)
    else:
        early = here * 3 // 4
        sends = [((None,), dc, 0, here * stations) for dc in range(chans)]
        sends += [((dz,), dc, 0, early) for dz in (2, 3) for dc in range(chans)]
        sent = make_spectra(frames_first, taps, tuple(sends), stations, chans, True)
        near = [shifted(sent[dc], stations, chans, 0, dc) if dc else sent[0] for dc in range(chans)]
        far = {}
        for ((dz,), dc, _, _), value in zip(sends[chans:], sent[chans:]):
            far[dz, dc] = shifted(value, stations, chans, dz, dc)
        cuts = ((2, early, here - early), (3, early, here - early), (1, 0, here))
        packed = pack(near, cuts, here)
        late = {}
        for (dz, _, _), value in zip(cuts, packed):
            late[dz] = shifted(value, stations, chans, dz, 0)
        whole = here * stations
        stages = ((0, whole // 2), (whole // 2, whole))
        pieces = [(dc, 0, dc, 0, at, at, last - at) for at, last in stages for dc in range(chans)]
        (own,) = correlate_pieces(near, pieces, stages, 1, chans, (0,), scale)
        parts, places = [], []
        for chunk, (first, last) in enumerate(((0, early), (early, here))):
            middle = (last - first) // 2
            stages = ((0, middle), (middle, last - first))
            arrays, pieces = list(near), []
            for at, end in stages:
                pieces += [(dc, 0, dc, here, first + at, at, end - at) for dc in range(chans)]
            for (dz, dc), value in far.items() if chunk == 0 else ():
                pieces += [(len(arrays), dz, dc, 0, at, at, end - at) for at, end in stages]
                arrays.append(value)
            for dz, value in late.items():
                if dz == 1 or chunk:
                    skip = first if dz == 1 else 0
                    pieces += [(len(arrays), dz, None, 0, skip + at, at, end - at) for at, end in stages]
                    arrays.append(value)
            outs = correlate_pieces(arrays, pieces, stages, stations, chans, tuple(range(1, reach)), scale)
            for dz in range(stations):
                parts.append(outs[dz] if dz == 0 else shifted(outs[dz], stations, chans, dz, 0))
                places.append((dz, first))
        out = assemble(own, parts, tuple(places), here)
    out = out.reshape(reach, stations * here, pairs // LANES, 2, LANES)
    return out.transpose(0, 1, 3, 2, 4).reshape(1, reach, stations * here, 2, pairs)


HALVES = 1


def direct(stations, chans):
    return stations == 4 and chans in (1, 2, 4)


def solution(mesh):
    placed = (P(("grp", "stn", "chan"), None, None), P())

    return jax.shard_map(
        local,
        mesh=mesh,
        in_specs=placed,
        out_specs=P(("grp", "stn"), None, "chan", None, None),
        check_vma=False,
    )
```
